1024 devices in a mesh: expert: 64 (over y, z), section: 16 (over x, core).
Axes of the slice: x: 8, y: 8, z: 8, core: 2. Of those that a mesh axis runs over, the one named last changes fastest.
Arguments:
- section_acts: bfloat16 [16, 12288, 256], P('section', 'expert'), may hold values from -6 to 6
- section_input_gradients: bfloat16 [16, 12288, 256], P('section', 'expert'), may hold values from -6 to 6
- saved_input: bfloat16 [16, 12288, 256], P('section', 'expert'), may hold values from -6 to 6
- fwd_routes: int32 [16, 768, 8], P('section'), may hold values from 0 to 255, all different within a row; in each aligned block of 192 rows (0 to 191, 192 to 383, ..., all dimensions but the last counted through in order) at most 12 rows name the same one
- fwd_probs: float32 [16, 768, 8], P('section'), may hold values from 0.1 to 1
- back_routes: int32 [16, 768, 8], P('section'), may hold values from 0 to 255, all different within a row; in each aligned block of 192 rows (0 to 191, 192 to 383, ..., all dimensions but the last counted through in order) at most 12 rows name the same one
- back_probs: float32 [16, 768, 8], P('section'), may hold values from 0.1 to 1
- w_gate: bfloat16 [16, 8192, 4096], P('section', 'expert'), may hold values from -0.09375 to 0.09375
- w_up: bfloat16 [16, 8192, 4096], P('section', 'expert'), may hold values from -0.09375 to 0.09375
- w_down: bfloat16 [16, 8192, 4096], P('section', 'expert'), may hold values from -0.125 to 0.125
Outputs:
- section_out: bfloat16 [16, 12288, 256], P('section', 'expert')
- input_grads: bfloat16 [16, 12288, 256], P('section', 'expert')
The draws below stay inside these ranges and needn't reach their ends.
Inputs may be any that keep to these rules, and one draw needn't show every extreme that they name: `fwd_routes`: in each aligned block of 192 rows (one group of one section) no id is named by more than 12 rows, and some block has an id named by exactly 12; every id is named somewhere. `back_routes`: in each aligned block of 192 rows (one group of one section) no id is named by more than 12 rows, and some block has an id named by exactly 12; every id is named somewhere.
All inputs are finite; a program needn't handle non-finite values.
Results may differ from the reference program's by a relative error of at most 0.0075.
Values may be sent and summed in bfloat16 or wider, within the bound.
A program may use at most 32 MiB of HBM per device.

```python
import math
import jax
import jax.numpy as jnp
import numpy as np
from jax import lax

D = 4096
F = 2048
N_ROUTED = 256
TOP = 8
E_WIN = 4
TOK_G = 192
DS = 256
CAP = 12
TOKENS = 768
ROWS = 12288
FW = 8192
N_EXPERT = 64
N_SECTION = 16


def levels(key, extent, cuts, least, high):
    def one(axis_at, blocks):
        draws = jax.random.uniform(jax.random.fold_in(jax.random.fold_in(key, 6), axis_at), (blocks,), jnp.float32, least / len(cuts), high / len(cuts))
        return jnp.repeat(jnp.exp(draws), extent[axis_at] // blocks).reshape((-1,) + (1,) * (len(extent) - axis_at - 1))

    loudness = one(*cuts[0])
    for cut in cuts[1:]:
        loudness = loudness * one(*cut)
    return loudness


def deal_out(key, own, number, rows, number_of, top, bound, skew):
    order = jax.random.permutation(key, number_of)
    heavy_load, ordinary = load_shares(number_of, rows * top, bound, skew, True), load_shares(number_of, rows * top, bound, skew, False)
    places = jnp.arange(number_of)

    def named(lengths, turn):
        used = int((lengths > 0).sum())
        fixed = max(1, used // 4)
        moved = fixed + (places - fixed + turn * (used - fixed)) % max(1, number_of - fixed)
        return jnp.zeros((number_of,), jnp.int32).at[order[jnp.where(places < fixed, places, moved)]].set(jnp.asarray(lengths, jnp.int32))

    lengths = jnp.where(number % 4 == 0, named(heavy_load, number // 4), named(ordinary, number - number // 4 - 1))
    mixed = jax.random.permutation(jax.random.fold_in(own, 3), number_of)
    donor, taker = mixed[0:number_of // 2 * 2:2], mixed[1:number_of // 2 * 2:2]
    room = jnp.minimum(lengths[donor] - 1, bound - lengths[taker]) // 2
    room = jnp.where((donor == order[0]) | (taker == order[0]) | (lengths[taker] == 0), 0, jnp.maximum(room, 0))
    moved = jax.random.randint(jax.random.fold_in(own, 4), (number_of // 2,), 0, 1 << 20) % (room + 1)
    lengths = lengths.at[donor].add(-moved).at[taker].add(moved)
    items = jnp.searchsorted(jnp.cumsum(lengths), jnp.arange(rows * top), side="right").astype(jnp.int32)
    grid = items.reshape(top, rows).T
    grid = grid[jax.random.permutation(jax.random.fold_in(own, 1), rows)]
    turn = jax.random.randint(jax.random.fold_in(own, 2), (rows, 1), 0, top)
    return jnp.take_along_axis(grid, (jnp.arange(top)[None, :] + turn) % top, axis=1)


def load_shares(count, total, limit, lean, full):
    weights = [(1 << 20) // math.isqrt(standing ** lean) + 1 for standing in range(1, count + 1)]
    largest = limit if full else min(limit, max(-(-total // count), total * weights[0] // sum(weights)))
    least = 1 if total - largest >= count - 1 else 0
    given, rest = [largest] + [least] * (count - 1), total - largest - least * (count - 1)
    while rest > 0:
        candidates = [i for i in range(1, count) if given[i] < largest] or [i for i in range(1, count) if given[i] < limit]
        mass, budget = sum([weights[i] for i in candidates]), rest
        for i in candidates:
            extra = min(limit - given[i], max(1, budget * weights[i] // mass), rest)
            given[i] = given[i] + extra
            rest = rest - extra
    return np.array(given)


def noise(own_key, shape, spread, most, shards=(), held_as=jnp.bfloat16):
    result = spread * jax.random.normal(own_key, shape, jnp.float32)
    if shards:
        result = result * levels(own_key, shape, shards, -0.22, 0.18)
    return jnp.clip(result, -most, most).astype(held_as)


def setup_inputs(seed: int = 0) -> dict:
    key_list = jax.random.split(jax.random.key(seed), 11)
    section_acts = noise(key_list[0], (N_SECTION, ROWS, DS), 1.0, 6.0, ((0, 16), (1, 64)))
    section_input_gradients = noise(key_list[1], (N_SECTION, ROWS, DS), 1.0, 6.0, ((0, 16), (1, 64)))
    saved_input = noise(key_list[2], (N_SECTION, ROWS, DS), 1.0, 6.0, ((0, 16), (1, 64)))
    fwd_routes_keys = jax.random.split(jax.random.fold_in(key_list[3], 1), N_SECTION * TOKENS // TOK_G)
    fwd_routes_turns = jax.random.permutation(jax.random.fold_in(key_list[3], 3), N_SECTION * TOKENS // TOK_G)
    fwd_routes = jax.vmap(lambda own, number: deal_out(jax.random.fold_in(key_list[3], 2), own, number, TOK_G, N_ROUTED, TOP, CAP, 2))(fwd_routes_keys, fwd_routes_turns).reshape((N_SECTION, TOKENS, TOP))
    fwd_probs = jnp.clip(jnp.exp(math.log(1.0) - 2.3025851 * jax.random.uniform(key_list[4], (N_SECTION, TOKENS, TOP), jnp.float32) ** levels(key_list[4], (N_SECTION, TOKENS, TOP), ((0, 16),), -0.2, 0.2)), 0.1, 1.0)
    back_routes_keys = jax.random.split(jax.random.fold_in(key_list[5], 1), N_SECTION * TOKENS // TOK_G)
    back_routes_turns = jax.random.permutation(jax.random.fold_in(key_list[5], 3), N_SECTION * TOKENS // TOK_G)
    back_routes = jax.vmap(lambda own, number: deal_out(jax.random.fold_in(key_list[5], 2), own, number, TOK_G, N_ROUTED, TOP, CAP, 2))(back_routes_keys, back_routes_turns).reshape((N_SECTION, TOKENS, TOP))
    back_probs = jnp.clip(jnp.exp(math.log(1.0) - 2.3025851 * jax.random.uniform(key_list[6], (N_SECTION, TOKENS, TOP), jnp.float32) ** levels(key_list[6], (N_SECTION, TOKENS, TOP), ((0, 16),), -0.2, 0.2)), 0.1, 1.0)
    w_gate = noise(key_list[7], (N_SECTION, FW, D), D ** -0.5, 0.09375, ((0, 16), (1, 64)))
    w_up = noise(key_list[8], (N_SECTION, FW, D), D ** -0.5, 0.09375, ((0, 16), (1, 64)))
    w_down = noise(key_list[9], (N_SECTION, FW, D), F ** -0.5, 0.125, ((0, 16), (1, 64)))
    return {"section_acts": section_acts, "section_input_gradients": section_input_gradients, "saved_input": saved_input, "fwd_routes": fwd_routes, "fwd_probs": fwd_probs, "back_routes": back_routes, "back_probs": back_probs, "w_gate": w_gate, "w_up": w_up, "w_down": w_down}


def tables(block, gains):
    labels = jnp.arange(E_WIN, dtype=jnp.int32)
    hits = block[:, :, None] == labels[None, None, :]
    chosen = jnp.sum(hits.astype(jnp.int32), axis=1, dtype=jnp.int32)
    weight = jnp.sum(jnp.where(hits, gains[:, :, None], jnp.float32(0.0)), axis=1)
    before = jnp.cumsum(chosen, axis=0, dtype=jnp.int32) - chosen
    places = jnp.arange(CAP, dtype=jnp.int32)
    mask = (before[:, None, :] == places[None, :, None]) & (chosen[:, None, :] > 0)
    picker = mask.astype(jnp.float32).reshape(block.shape[0], CAP * E_WIN)
    weighted = jnp.where(mask, weight[:, None, :], jnp.float32(0.0)).reshape(block.shape[0], CAP * E_WIN)
    return picker, weighted


def reference(section_acts, section_input_gradients, saved_input, fwd_routes, fwd_probs, back_routes, back_probs, w_gate, w_up, w_down):
    split = N_EXPERT // E_WIN
    hid = F // split
    high = lax.Precision.HIGHEST

    def unblock(values_array):
        cols = values_array.shape[1]
        return values_array.reshape(E_WIN, split, TOK_G, cols).transpose(0, 2, 1, 3).reshape(E_WIN, TOK_G, split * cols)

    def regroup_blocks(values_array):
        cols = D // split
        return values_array.reshape(E_WIN, TOK_G, split, cols).transpose(0, 2, 1, 3).reshape(E_WIN * split * TOK_G, cols)

    def to_experts(rows):
        return rows.reshape(E_WIN, CAP, E_WIN, D).transpose(2, 0, 1, 3).reshape(E_WIN, E_WIN * CAP, D)

    def to_groups(rows):
        return rows.reshape(E_WIN, E_WIN, CAP, D).transpose(1, 2, 0, 3).reshape(E_WIN, CAP * E_WIN, D)

    def one_section(items):
        acts, grads, saved, f_routes, f_probs, b_routes, b_probs, gate_w, up_w, down_w = items
        x_in = unblock(acts)
        dy_in = unblock(grads)
        backward_input = unblock(saved)
        f_pick, f_weight = jax.vmap(tables)(f_routes.reshape(E_WIN, TOK_G, TOP), f_probs.reshape(E_WIN, TOK_G, TOP))
        b_pick, b_weight = jax.vmap(tables)(b_routes.reshape(E_WIN, TOK_G, TOP), b_probs.reshape(E_WIN, TOK_G, TOP))
        gate_e = gate_w.reshape(E_WIN, split, hid, D).astype(jnp.float32)
        up_e = up_w.reshape(E_WIN, split, hid, D).astype(jnp.float32)
        down_e = down_w.reshape(E_WIN, split, hid, D).astype(jnp.float32)

        f_rows = jnp.einsum('gtm,gtd->gmd', f_pick, x_in.astype(jnp.float32), precision=high).astype(jnp.bfloat16)
        f_rows = to_experts(f_rows).astype(jnp.float32)
        gate_pre = jnp.einsum('erd,eshd->ersh', f_rows, gate_e, precision=high)
        up_pre = jnp.einsum('erd,eshd->ersh', f_rows, up_e, precision=high)
        hidden = (jax.nn.silu(gate_pre) * up_pre).astype(jnp.bfloat16)
        part = jnp.einsum('ersh,eshd->esrd', hidden.astype(jnp.float32), down_e, precision=high).astype(jnp.bfloat16)
        made = jnp.sum(part.astype(jnp.float32), axis=1)
        moe = jnp.einsum('gtm,gmd->gtd', f_weight, to_groups(made), precision=high)
        layer_output = (x_in.astype(jnp.float32) + moe).astype(jnp.bfloat16)

        scale = jnp.sum(b_weight, axis=1)
        b_rows = jnp.einsum('gtm,gtd->gmd', b_pick, backward_input.astype(jnp.float32), precision=high).astype(jnp.bfloat16)
        g_rows = jnp.einsum('gtm,gtd->gmd', b_pick, dy_in.astype(jnp.float32), precision=high)
        g_rows = (g_rows * scale[:, :, None]).astype(jnp.bfloat16)
        b_rows = to_experts(b_rows).astype(jnp.float32)
        g_rows = to_experts(g_rows).astype(jnp.float32)
        gate_b = jnp.einsum('erd,eshd->ersh', b_rows, gate_e, precision=high)
        up_b = jnp.einsum('erd,eshd->ersh', b_rows, up_e, precision=high)
        sig = jax.nn.sigmoid(gate_b)
        act = gate_b * sig
        d_hidden = jnp.einsum('erd,eshd->ersh', g_rows, down_e, precision=high)
        d_up = (d_hidden * act).astype(jnp.bfloat16).astype(jnp.float32)
        d_gate = (d_hidden * up_b * sig * (1.0 + gate_b * (1.0 - sig))).astype(jnp.bfloat16).astype(jnp.float32)
        back = jnp.einsum('ersh,eshd->esrd', d_gate, gate_e, precision=high) + jnp.einsum('ersh,eshd->esrd', d_up, up_e, precision=high)
        back = jnp.sum(back.astype(jnp.bfloat16).astype(jnp.float32), axis=1)
        dx_moe = jnp.einsum('gtm,gmd->gtd', b_pick, to_groups(back), precision=high)
        input_gradient = (dy_in.astype(jnp.float32) + dx_moe).astype(jnp.bfloat16)
        return regroup_blocks(layer_output), regroup_blocks(input_gradient)

    acts_all = jnp.roll(section_acts, 1, axis=0)
    grads_all = jnp.roll(section_input_gradients, -1, axis=0)
    section_out, input_grads = lax.map(one_section, (acts_all, grads_all, saved_input, fwd_routes, fwd_probs, back_routes, back_probs, w_gate, w_up, w_down))
    return section_out, input_grads
```

```python
import jax
import jax.numpy as jnp
from jax import lax
from jax.experimental import pallas as pl
from jax.experimental.pallas import tpu as pltpu
from jax.sharding import PartitionSpec as P

MESH = pl.DeviceIdType.MESH
BF16 = jnp.bfloat16
F32 = jnp.float32

TOP = 8
E_WIN = 4
Z = 8
Y = 8
TOK = 192
DS = 256
CAP = 12
PAD = 16
SLOTS = E_WIN * PAD
ROWS = E_WIN * CAP
HID = 128
HALF = Z * DS
X, G, B = 1, 2, 0


def dot_nt(a, b):
    return lax.dot_general(a, b, (((1,), (1,)), ((), ())), preferred_element_type=F32)


def dot_nn(a, b):
    return lax.dot_general(a, b, (((1,), (0,)), ((), ())), preferred_element_type=F32)


def dot_tn(a, b):
    return lax.dot_general(a, b, (((0,), (0,)), ((), ())), preferred_element_type=F32)


def own_tokens(whole, group):
    block = whole[:, 0:TOK]
    for g in range(1, E_WIN):
        block = jnp.where(group == g, whole[:, g * TOK : (g + 1) * TOK], block)
    return block


def pickers(routes, probs, group, before_ref):
    routes = own_tokens(routes, group)
    probs = own_tokens(probs, group)
    slot = lax.broadcasted_iota(jnp.int32, (SLOTS, TOK), 0)
    expert = slot // PAD
    chosen = jnp.zeros((SLOTS, TOK), F32)
    weight = jnp.zeros((SLOTS, TOK), F32)
    for e in range(E_WIN):
        hit = routes == e
        named = jnp.sum(jnp.where(hit, 1.0, 0.0), axis=0, keepdims=True)
        gain = jnp.sum(jnp.where(hit, probs, 0.0), axis=0, keepdims=True)
        chosen = jnp.where(expert == e, jnp.broadcast_to(named, (SLOTS, TOK)), chosen)
        weight = jnp.where(expert == e, jnp.broadcast_to(gain, (SLOTS, TOK)), weight)
    before = dot_nn(chosen.astype(BF16), before_ref[...])
    place = (slot - expert * PAD).astype(F32)
    mask = (before == place) & (chosen > 0.5)
    picker = jnp.where(mask, 1.0, 0.0).astype(BF16)
    column = jnp.sum(jnp.where(mask, weight, 0.0), axis=1, keepdims=True)
    return picker, column


def kernel(
    acts,
    grads,
    saved,
    f_routes,
    f_probs,
    b_routes,
    b_probs,
    w_gate,
    w_up,
    w_down,
    out,
    out_grads,
    relay,
    kept,
    routes,
    probs,
    wgu,
    wd,
    earlier,
    pick,
    ex,
    rows,
    ring_out,
    ring_in,
    fin,
    comb,
    local_sem,
    relay_sem,
    ex_send,
    ex_recv,
    ag_send,
    ag_recv,
    rs_send,
    rs_recv,
    fin_send,
    fin_recv,
):
    me = lax.axis_index("expert")
    section = lax.axis_index("section")
    sections = lax.axis_size("section")
    y = me // Z
    z = me % Z
    g = y // 2
    r = y % 2
    up = y * Z + (z + 1) % Z
    down = y * Z + (z + Z - 1) % Z
    after = (section + 1) % sections
    behind = (section + sections - 1) % sections
    columns = [((y + d) % Y) * Z + z for d in range(Y)]

    barrier = pltpu.get_barrier_semaphore()
    for d in (4, 3, 5, 2, 6, 1, 7):
        pl.semaphore_signal(barrier, inc=1, device_id={"expert": columns[d]}, device_id_type=MESH)
    for peer in (up, down):
        pl.semaphore_signal(barrier, inc=1, device_id={"expert": peer}, device_id_type=MESH)
    for peer in (after, behind):
        pl.semaphore_signal(barrier, inc=1, device_id={"section": peer}, device_id_type=MESH)

    loads = [
        pltpu.make_async_copy(b_routes, routes.at[1], local_sem.at[0]),
        pltpu.make_async_copy(b_probs, probs.at[1], local_sem.at[1]),
        pltpu.make_async_copy(saved, kept, local_sem.at[2]),
        pltpu.make_async_copy(f_routes, routes.at[0], local_sem.at[3]),
        pltpu.make_async_copy(f_probs, probs.at[0], local_sem.at[4]),
        pltpu.make_async_copy(w_gate, wgu.at[pl.ds(0, HID)], local_sem.at[5]),
        pltpu.make_async_copy(w_up, wgu.at[pl.ds(HID, HID)], local_sem.at[6]),
        pltpu.make_async_copy(w_down, wd, local_sem.at[7]),
    ]
    for load in loads:
        load.start()

    t0 = lax.broadcasted_iota(jnp.int32, (TOK, TOK), 0)
    t1 = lax.broadcasted_iota(jnp.int32, (TOK, TOK), 1)
    earlier[...] = jnp.where(t0 < t1, 1.0, 0.0).astype(BF16)
    slot = lax.broadcasted_iota(jnp.int32, (ROWS, SLOTS), 1)
    row = lax.broadcasted_iota(jnp.int32, (ROWS, SLOTS), 0)
    packer = jnp.where(row == (slot // PAD) * CAP + slot % PAD, jnp.where(slot % PAD < CAP, 1.0, 0.0), 0.0).astype(BF16)
    wide = lax.broadcasted_iota(jnp.int32, (SLOTS, ROWS), 0)
    long = lax.broadcasted_iota(jnp.int32, (SLOTS, ROWS), 1)
    unpacker = jnp.where(long == (wide // PAD) * CAP + wide % PAD, jnp.where(wide % PAD < CAP, 1.0, 0.0), 0.0).astype(BF16)

    def expert_slots(e):
        return pl.ds(pl.multiple_of(e * PAD, PAD), PAD)

    ex_copies = {}

    def exchange(d):
        ex[d, r, expert_slots(g), :] = pick[d, expert_slots(g), :]
        for s in (4, 3, 5, 2, 6, 1, 7):
            ex_copies[d, s] = pltpu.make_async_remote_copy(
                src_ref=pick.at[d, expert_slots(((y + s) % Y) // 2)],
                dst_ref=ex.at[d, r, expert_slots(g)],
                send_sem=ex_send.at[d, s],
                recv_sem=ex_recv.at[d, s],
                device_id={"expert": columns[s]},
                device_id_type=MESH,
            )
            ex_copies[d, s].start()

    def gather_own(d):
        for s in (1, 7, 2, 6, 3, 5, 4):
            ex_copies[d, s].wait_recv()
        for half in range(2):
            rows[d, z, half] = dot_nn(packer, ex[d, half]).astype(BF16)

    ag_copies = {}

    def pass_on(d, hop):
        for way in range(2):
            block = (z + Z - hop) % Z if way == 0 else (z + hop) % Z
            part = rows.at[d, block] if hop < 3 else rows.at[d, block, way]
            ag_copies[d, way, hop] = pltpu.make_async_remote_copy(
                src_ref=part,
                dst_ref=part,
                send_sem=ag_send.at[d, way, hop],
                recv_sem=ag_recv.at[d, way, hop],
                device_id={"expert": up if way == 0 else down},
                device_id_type=MESH,
            )
            ag_copies[d, way, hop].start()

    def arrived(d, hop):
        for way in range(2):
            ag_copies[d, way, hop].wait_recv()

    def features(block, half):
        return pl.ds(pl.multiple_of(half * HALF + block * DS, DS), DS)

    def into(d, block, total):
        for half in range(2):
            weights = wd if d == G else wgu
            term = dot_nt(rows[d, block, half], weights[:, features(block, half)])
            total = term if total is None else total + term
        return total

    totals = {B: None, X: None, G: None}

    def absorb(d, hop):
        if hop < 0:
            blocks = (z,)
        elif hop < 3:
            blocks = ((z + Z - hop - 1) % Z, (z + hop + 1) % Z)
        else:
            blocks = ((z + 4) % Z,)
        for block in blocks:
            totals[d] = into(d, block, totals[d])

    for load in loads[:3]:
        load.wait()
    b_picker, b_column = pickers(routes[1], probs[1], g, earlier)
    pick[B] = dot_nn(b_picker, kept[...]).astype(BF16)

    pl.semaphore_wait(barrier, 11)

    relays = [
        pltpu.make_async_remote_copy(
            src_ref=source,
            dst_ref=relay.at[i],
            send_sem=relay_sem.at[i],
            recv_sem=relay_sem.at[2 + i],
            device_id={"section": peer},
            device_id_type=MESH,
        )
        for i, (source, peer) in enumerate(((acts, after), (grads, behind)))
    ]
    for copy in relays:
        copy.start()
    exchange(B)

    for load in loads[3:5]:
        load.wait()
    f_picker, f_column = pickers(routes[0], probs[0], g, earlier)

    relays[0].wait_recv()
    pick[X] = dot_nn(f_picker, relay[0]).astype(BF16)
    exchange(X)
    relays[1].wait_recv()
    pick[G] = (dot_nn(b_picker, relay[1]) * b_column).astype(BF16)
    exchange(G)

    for load in loads[5:]:
        load.wait()

    gather_own(B)
    pass_on(B, 0)
    absorb(B, -1)
    gather_own(X)
    pass_on(X, 0)
    absorb(X, -1)
    arrived(B, 0)
    pass_on(B, 1)
    gather_own(G)
    pass_on(G, 0)
    absorb(B, 0)
    absorb(G, -1)
    for d, hop in ((X, 0), (B, 1), (G, 0), (X, 1), (B, 2), (G, 1), (X, 2)):
        arrived(d, hop)
        pass_on(d, hop + 1)
        absorb(d, hop)
    arrived(B, 3)
    absorb(B, 3)
    arrived(G, 2)
    pass_on(G, 3)
    absorb(G, 2)

    rs_copies = {}

    def own_part(c, block, half):
        if c == 0:
            return dot_nn(made[0], wd[:, features(block, half)])
        return dot_nn(made[1], wgu[:, features(block, half)])

    def reduce_step(c, step):
        for way in range(2):
            block = (z + 4 - step) % Z if way == 0 else (z + 4 + step) % Z
            if step > 0:
                rs_copies[c, way, step - 1].wait_recv()
            for half in range(2):
                if step == 0 and half != way:
                    continue
                value = own_part(c, block, half)
                if step > 1 or (step == 1 and half == way):
                    value = value + ring_in[c, way, step - 1, half].astype(F32)
                ring_out[c, way, step, half] = value.astype(BF16)
            at = (c, way, step) if step > 0 else (c, way, step, way)
            rs_copies[c, way, step] = pltpu.make_async_remote_copy(
                src_ref=ring_out.at[at],
                dst_ref=ring_in.at[at],
                send_sem=rs_send.at[c, way, step],
                recv_sem=rs_recv.at[c, way, step],
                device_id={"expert": up if way == 0 else down},
                device_id_type=MESH,
            )
            rs_copies[c, way, step].start()

    fin_copies = {}

    def send_back(c):
        for way in range(2):
            rs_copies[c, way, 3].wait_recv()
        for half in range(2):
            value = own_part(c, z, half)
            for way in range(2):
                value = value + ring_in[c, way, 3, half].astype(F32)
            fin[c, half] = dot_nn(unpacker, value.astype(BF16)).astype(BF16)
        comb[c, r, expert_slots(g), :] = fin[c, r, expert_slots(g), :]
        for s in (4, 3, 5, 2, 6, 1, 7):
            to = (y + s) % Y
            fin_copies[c, s] = pltpu.make_async_remote_copy(
                src_ref=fin.at[c, to % 2, expert_slots(to // 2)],
                dst_ref=comb.at[c, r, expert_slots(g)],
                send_sem=fin_send.at[c, s],
                recv_sem=fin_recv.at[c, s],
                device_id={"expert": columns[s]},
                device_id_type=MESH,
            )
            fin_copies[c, s].start()

    def place(picker, values):
        high = values.astype(BF16)
        low = (values - high.astype(F32)).astype(BF16)
        return dot_tn(picker, high) + dot_tn(picker, low)

    def finish(c, picker, column, base, target):
        for s in (1, 7, 2, 6, 3, 5, 4):
            fin_copies[c, s].wait_recv()
        values = comb[c, 0].astype(F32) + comb[c, 1].astype(F32)
        if column is not None:
            values = values * column
        target[...] = (base.astype(F32) + place(picker, values)).astype(BF16)

    made = {}

    arrived(X, 3)
    absorb(X, 3)
    gate, upper = totals[X][:, :HID], totals[X][:, HID:]
    made[0] = (gate * jax.nn.sigmoid(gate) * upper).astype(BF16)
    reduce_step(0, 0)

    gate, upper = totals[B][:, :HID], totals[B][:, HID:]
    sig = jax.nn.sigmoid(gate)
    act = gate * sig
    slope = upper * sig * (1.0 + gate * (1.0 - sig))
    arrived(G, 3)
    absorb(G, 3)
    d_hidden = totals[G]
    made[1] = jnp.concatenate([(d_hidden * slope).astype(BF16), (d_hidden * act).astype(BF16)], axis=1)
    reduce_step(1, 0)
    for step in range(1, 4):
        reduce_step(0, step)
        reduce_step(1, step)
    send_back(0)
    send_back(1)
    finish(0, f_picker, f_column, relay[0], out)
    finish(1, b_picker, None, relay[1], out_grads)

    for copies in (relays, ex_copies.values(), ag_copies.values(), rs_copies.values(), fin_copies.values()):
        for copy in copies:
            copy.wait_send()


def tick(section_acts, section_input_gradients, saved_input, fwd_routes, fwd_probs, back_routes, back_probs, w_gate, w_up, w_down):
    anywhere = pl.BlockSpec(memory_space=pl.ANY)
    inside = pl.BlockSpec(memory_space=pltpu.VMEM)
    block = jax.ShapeDtypeStruct((TOK, DS), BF16)
    dma = pltpu.SemaphoreType.DMA
    out, out_grads = pl.pallas_call(
        kernel,
        out_shape=(block, block),
        in_specs=[anywhere] * 10,
        out_specs=(inside, inside),
        scratch_shapes=[
            pltpu.VMEM((2, TOK, DS), BF16),
            pltpu.VMEM((TOK, DS), BF16),
            pltpu.VMEM((2, TOP, E_WIN * TOK), jnp.int32),
            pltpu.VMEM((2, TOP, E_WIN * TOK), F32),
            pltpu.VMEM((2 * HID, 2 * HALF), BF16),
            pltpu.VMEM((HID, 2 * HALF), BF16),
            pltpu.VMEM((TOK, TOK), BF16),
            pltpu.VMEM((3, SLOTS, DS), BF16),
            pltpu.VMEM((3, 2, SLOTS, DS), BF16),
            pltpu.VMEM((3, Z, 2, ROWS, DS), BF16),
            pltpu.VMEM((2, 2, 4, 2, ROWS, DS), BF16),
            pltpu.VMEM((2, 2, 4, 2, ROWS, DS), BF16),
            pltpu.VMEM((2, 2, SLOTS, DS), BF16),
            pltpu.VMEM((2, 2, SLOTS, DS), BF16),
            dma((8,)),
            dma((4,)),
            dma((3, Y)),
            dma((3, Y)),
            dma((3, 2, 4)),
            dma((3, 2, 4)),
            dma((2, 2, 4)),
            dma((2, 2, 4)),
            dma((2, Y)),
            dma((2, Y)),
        ],
        compiler_params=pltpu.CompilerParams(collective_id=0, has_side_effects=True),
    )(
        section_acts[0],
        section_input_gradients[0],
        saved_input[0],
        fwd_routes[0].T,
        fwd_probs[0].T,
        back_routes[0].T,
        back_probs[0].T,
        w_gate[0],
        w_up[0],
        w_down[0],
    )
    return out[None], out_grads[None]


def solution(mesh):
    spread = P("section", "expert", None)
    whole = P("section", None, None)
    return jax.shard_map(
        tick,
        mesh=mesh,
        in_specs=(spread, spread, spread, whole, whole, whole, whole, spread, spread, spread),
        out_specs=(spread, spread),
        check_vma=False,
    )
```

```python
import jax
import jax.numpy as jnp
from jax import lax
from jax.experimental import pallas as pl
from jax.experimental.pallas import tpu as pltpu
from jax.sharding import PartitionSpec as P

MESH = pl.DeviceIdType.MESH
BF16 = jnp.bfloat16
F32 = jnp.float32

TOP = 8
E_WIN = 4
Z = 8
Y = 8
TOK = 192
DS = 256
CAP = 12
PAD = 16
SLOTS = E_WIN * PAD
ROWS = E_WIN * CAP
HID = 128
HALF = Z * DS
X, G, B = 1, 2, 0
LONG, SHORT = 0, 4


def dot_nt(a, b):
    return lax.dot_general(a, b, (((1,), (1,)), ((), ())), preferred_element_type=F32)


def dot_nn(a, b):
    return lax.dot_general(a, b, (((1,), (0,)), ((), ())), preferred_element_type=F32)


def dot_tn(a, b):
    return lax.dot_general(a, b, (((0,), (0,)), ((), ())), preferred_element_type=F32)


def own_tokens(whole, group):
    block = whole[:, 0:TOK]
    for g in range(1, E_WIN):
        block = jnp.where(group == g, whole[:, g * TOK : (g + 1) * TOK], block)
    return block


def pickers(routes, probs, group, before_ref):
    routes = own_tokens(routes, group)
    probs = own_tokens(probs, group)
    slot = lax.broadcasted_iota(jnp.int32, (SLOTS, TOK), 0)
    expert = slot // PAD
    chosen = jnp.zeros((SLOTS, TOK), F32)
    weight = jnp.zeros((SLOTS, TOK), F32)
    for e in range(E_WIN):
        hit = routes == e
        named = jnp.sum(jnp.where(hit, 1.0, 0.0), axis=0, keepdims=True)
        gain = jnp.sum(jnp.where(hit, probs, 0.0), axis=0, keepdims=True)
        chosen = jnp.where(expert == e, jnp.broadcast_to(named, (SLOTS, TOK)), chosen)
        weight = jnp.where(expert == e, jnp.broadcast_to(gain, (SLOTS, TOK)), weight)
    before = dot_nn(chosen.astype(BF16), before_ref[...])
    place = (slot - expert * PAD).astype(F32)
    mask = (before == place) & (chosen > 0.5)
    picker = jnp.where(mask, 1.0, 0.0).astype(BF16)
    column = jnp.sum(jnp.where(mask, weight, 0.0), axis=1, keepdims=True)
    return picker, column


def before_mask():
    t0 = lax.broadcasted_iota(jnp.int32, (TOK, TOK), 0)
    t1 = lax.broadcasted_iota(jnp.int32, (TOK, TOK), 1)
    return jnp.where(t0 < t1, 1.0, 0.0).astype(BF16)


def pack_matrix(shape, slot_axis):
    slot = lax.broadcasted_iota(jnp.int32, shape, slot_axis)
    row = lax.broadcasted_iota(jnp.int32, shape, 1 - slot_axis)
    same = row == (slot // PAD) * CAP + slot % PAD
    return jnp.where(same, jnp.where(slot % PAD < CAP, 1.0, 0.0), 0.0).astype(BF16)


def identity():
    i = lax.broadcasted_iota(jnp.int32, (SLOTS, SLOTS), 0)
    j = lax.broadcasted_iota(jnp.int32, (SLOTS, SLOTS), 1)
    return jnp.where(i == j, 1.0, 0.0).astype(BF16)


def kernel(
    acts,
    grads,
    saved,
    f_routes,
    f_probs,
    b_routes,
    b_probs,
    w_gate,
    w_up,
    w_down,
    out,
    out_grads,
    relay,
    kept,
    routes,
    probs,
    wgu,
    wd,
    earlier,
    pick,
    ex,
    rows,
    parts,
    ring_out,
    ring_in,
    fin,
    comb,
    meter,
    local_sem,
    relay_sem,
    ex_send,
    ex_recv,
    ag_send,
    ag_recv,
    rs_send,
    rs_recv,
    fin_send,
    fin_recv,
):
    me = lax.axis_index("expert")
    section = lax.axis_index("section")
    sections = lax.axis_size("section")
    y = me // Z
    z = me % Z
    g = y // 2
    r = y % 2
    up = y * Z + (z + 1) % Z
    down = y * Z + (z + Z - 1) % Z
    after = (section + 1) % sections
    behind = (section + sections - 1) % sections
    columns = [((y + d) % Y) * Z + z for d in range(Y)]

    barrier = pltpu.get_barrier_semaphore()
    for d in (4, 3, 5, 2, 6, 1, 7):
        pl.semaphore_signal(barrier, inc=1, device_id={"expert": columns[d]}, device_id_type=MESH)
    for peer in (up, down):
        pl.semaphore_signal(barrier, inc=1, device_id={"expert": peer}, device_id_type=MESH)
    for peer in (after, behind):
        pl.semaphore_signal(barrier, inc=1, device_id={"section": peer}, device_id_type=MESH)

    loads = [
        pltpu.make_async_copy(b_routes, routes.at[1], local_sem.at[0]),
        pltpu.make_async_copy(b_probs, probs.at[1], local_sem.at[1]),
        pltpu.make_async_copy(saved, kept, local_sem.at[2]),
        pltpu.make_async_copy(f_routes, routes.at[0], local_sem.at[3]),
        pltpu.make_async_copy(f_probs, probs.at[0], local_sem.at[4]),
        pltpu.make_async_copy(w_gate, wgu.at[pl.ds(0, HID)], local_sem.at[5]),
        pltpu.make_async_copy(w_up, wgu.at[pl.ds(HID, HID)], local_sem.at[6]),
        pltpu.make_async_copy(w_down, wd, local_sem.at[7]),
    ]
    for load in loads:
        load.start()

    def expert_slots(e):
        return pl.ds(pl.multiple_of(e * PAD, PAD), PAD)

    def all_of(like, sem):
        pltpu.make_async_copy(like, like, sem).wait()


    def exchange(d):
        ex[d, r, expert_slots(g), :] = pick[d, expert_slots(g), :]
        for s in (4, 3, 5, 2, 6, 1, 7):
            pltpu.make_async_remote_copy(
                src_ref=pick.at[d, expert_slots(((y + s) % Y) // 2)],
                dst_ref=ex.at[d, r, expert_slots(g)],
                send_sem=ex_send.at[d],
                recv_sem=ex_recv.at[d],
                device_id={"expert": columns[s]},
                device_id_type=MESH,
            ).start()

    def gather_own(d):
        all_of(meter, ex_recv.at[d])
        for half in range(2):
            rows[d, z, half] = dot_nn(packer, ex[d, half]).astype(BF16)
        pass_on(d, 0, LONG)
        pass_on(d, 0, SHORT)
        absorb(d, ((z, 0), (z, 1)))

    ag_copies = {}

    def pass_on(d, hop, chain):
        for way in range(2):
            half = way if chain == LONG else 1 - way
            block = (z + Z - hop) % Z if way == 0 else (z + hop) % Z
            piece = rows.at[d, block, half]
            copy = pltpu.make_async_remote_copy(
                src_ref=piece,
                dst_ref=piece,
                send_sem=ag_send.at[d],
                recv_sem=ag_recv.at[d, way, chain + hop],
                device_id={"expert": up if way == 0 else down},
                device_id_type=MESH,
            )
            if hop > 0:
                ag_copies[d, way, hop - 1, chain].wait_recv()
            ag_copies[d, way, hop, chain] = copy
            copy.start()

    def features(block, half):
        return pl.ds(pl.multiple_of(half * HALF + block * DS, DS), DS)

    totals = {B: None, X: None, G: None}

    def absorb(d, blocks):
        for block, half in blocks:
            weights = wd if d == G else wgu
            term = dot_nt(rows[d, block, half], weights[:, features(block, half)])
            totals[d] = term if totals[d] is None else totals[d] + term

    def arrived(d, hop, chain):
        if hop + 1 < (4 if chain == LONG else 3):
            pass_on(d, hop + 1, chain)
        else:
            for way in range(2):
                ag_copies[d, way, hop, chain].wait_recv()
        first, second = (0, 1) if chain == LONG else (1, 0)
        absorb(d, (((z + Z - hop - 1) % Z, first), ((z + hop + 1) % Z, second)))

    pl.semaphore_wait(barrier, 11)

    relays = [
        pltpu.make_async_remote_copy(
            src_ref=source,
            dst_ref=relay.at[i],
            send_sem=relay_sem.at[i],
            recv_sem=relay_sem.at[2 + i],
            device_id={"section": peer},
            device_id_type=MESH,
        )
        for i, (source, peer) in enumerate(((acts, after), (grads, behind)))
    ]
    for copy in relays:
        copy.start()

    earlier[...] = before_mask()
    for load in loads[:2]:
        load.wait()
    b_picker, b_column = pickers(routes[1], probs[1], g, earlier)
    loads[2].wait()
    pick[B] = dot_nn(b_picker, kept[...]).astype(BF16)
    exchange(B)
    for load in loads[3:5]:
        load.wait()
    f_picker, f_column = pickers(routes[0], probs[0], g, earlier)

    relays[0].wait_recv()
    pick[X] = dot_nn(f_picker, relay[0]).astype(BF16)
    exchange(X)
    relays[1].wait_recv()
    pick[G] = (dot_nn(b_picker, relay[1]) * b_column).astype(BF16)
    exchange(G)

    packer = pack_matrix((ROWS, SLOTS), 1)
    unpacker = pack_matrix((SLOTS, ROWS), 0)
    token_of = [dot_tn(p, identity()).astype(BF16) for p in (f_picker, b_picker)]

    for load in loads[5:]:
        load.wait()

    gather_own(B)
    gather_own(X)
    arrived(B, 0, LONG)
    arrived(B, 0, SHORT)
    gather_own(G)
    for d, hop in ((X, 0), (B, 1), (G, 0), (X, 1), (B, 2), (G, 1), (X, 2)):
        arrived(d, hop, LONG)
        arrived(d, hop, SHORT)
    arrived(B, 3, LONG)
    arrived(G, 2, LONG)
    arrived(G, 2, SHORT)

    rs_copies = {}

    def own_part(c, block, half):
        if c == 0:
            return dot_nn(made[0], wd[:, features(block, half)])
        return dot_nn(made[1], wgu[:, features(block, half)])

    def turns(turn):
        for way in range(2):
            yield way, way, turn
        if turn < 3:
            for way in range(2):
                yield way, 1 - way, turn + 1

    def own_parts(c, turn):
        for way, half, step in turns(turn):
            block = (z + 4 - step) % Z if way == 0 else (z + 4 + step) % Z
            parts[c, way, step, half] = own_part(c, block, half)

    def reduce_turn(c, turn):
        for way, half, step in turns(turn):
            value = parts[c, way, step, half]
            if turn > 0:
                rs_copies[c, way, half, turn - 1].wait_recv()
                value = value + ring_in[c, way, step - 1, half].astype(F32)
            ring_out[c, way, step, half] = value.astype(BF16)
            at = (c, way, step, half)
            copy = pltpu.make_async_remote_copy(
                src_ref=ring_out.at[at],
                dst_ref=ring_in.at[at],
                send_sem=rs_send.at[c],
                recv_sem=rs_recv.at[c, way, (LONG if half == way else SHORT) + turn],
                device_id={"expert": up if way == 0 else down},
                device_id_type=MESH,
            )
            rs_copies[c, way, half, turn] = copy
            copy.start()

    def send_back(c):
        mine = [own_part(c, z, half) for half in range(2)]
        for half in range(2):
            value = mine[half]
            for way in (1 - half, half):
                rs_copies[c, way, half, 3 if half == way else 2].wait_recv()
                value = value + ring_in[c, way, 3, half].astype(F32)
            fin[c, half] = dot_nn(unpacker, value.astype(BF16)).astype(BF16)
        comb[c, r, expert_slots(g), :] = fin[c, r, expert_slots(g), :]
        for s in (4, 3, 5, 2, 6, 1, 7):
            to = (y + s) % Y
            pltpu.make_async_remote_copy(
                src_ref=fin.at[c, to % 2, expert_slots(to // 2)],
                dst_ref=comb.at[c, r, expert_slots(g)],
                send_sem=fin_send.at[c],
                recv_sem=fin_recv.at[c],
                device_id={"expert": columns[s]},
                device_id_type=MESH,
            ).start()

    def place(picker, values):
        high = values.astype(BF16)
        low = (values - high.astype(F32)).astype(BF16)
        return dot_nn(picker, high) + dot_nn(picker, low)

    def finish(c, picker, column, base, target):
        all_of(meter, fin_recv.at[c])
        values = comb[c, 0].astype(F32) + comb[c, 1].astype(F32)
        if column is not None:
            values = values * column
        target[...] = (base.astype(F32) + place(picker, values)).astype(BF16)

    made = {}

    arrived(X, 3, LONG)
    gate, upper = totals[X][:, :HID], totals[X][:, HID:]
    made[0] = (gate * jax.nn.sigmoid(gate) * upper).astype(BF16)
    own_parts(0, 0)
    reduce_turn(0, 0)

    gate, upper = totals[B][:, :HID], totals[B][:, HID:]
    sig = jax.nn.sigmoid(gate)
    act = gate * sig
    slope = upper * sig * (1.0 + gate * (1.0 - sig))
    arrived(G, 3, LONG)
    d_hidden = totals[G]
    made[1] = jnp.concatenate([(d_hidden * slope).astype(BF16), (d_hidden * act).astype(BF16)], axis=1)
    own_parts(1, 0)
    reduce_turn(1, 0)
    for turn in range(1, 4):
        for c in range(2):
            own_parts(c, turn)
            reduce_turn(c, turn)
    send_back(0)
    send_back(1)
    finish(0, token_of[0], f_column, relay[0], out)
    finish(1, token_of[1], None, relay[1], out_grads)

    def drain():
        for copy in relays:
            copy.wait_send()
        for d in range(3):
            all_of(meter, ex_send.at[d])
            all_of(rows.at[d, pl.ds(0, 7)], ag_send.at[d])
        for c in range(2):
            all_of(rows.at[c, pl.ds(0, 7)], rs_send.at[c])
            all_of(meter, fin_send.at[c])

    drain()


def tick(section_acts, section_input_gradients, saved_input, fwd_routes, fwd_probs, back_routes, back_probs, w_gate, w_up, w_down):
    anywhere = pl.BlockSpec(memory_space=pl.ANY)
    inside = pl.BlockSpec(memory_space=pltpu.VMEM)
    block = pltpu.VMEM((TOK, DS), BF16)
    dma = pltpu.SemaphoreType.DMA
    out, out_grads = pl.pallas_call(
        kernel,
        out_shape=(block, block),
        in_specs=[anywhere] * 10,
        out_specs=(inside, inside),
        scratch_shapes=[
            pltpu.VMEM((2, TOK, DS), BF16),
            pltpu.VMEM((TOK, DS), BF16),
            pltpu.VMEM((2, TOP, E_WIN * TOK), jnp.int32),
            pltpu.VMEM((2, TOP, E_WIN * TOK), F32),
            pltpu.VMEM((2 * HID, 2 * HALF), BF16),
            pltpu.VMEM((HID, 2 * HALF), BF16),
            pltpu.VMEM((TOK, TOK), BF16),
            pltpu.VMEM((3, SLOTS, DS), BF16),
            pltpu.VMEM((3, 2, SLOTS, DS), BF16),
            pltpu.VMEM((3, Z, 2, ROWS, DS), BF16),
            pltpu.VMEM((2, 2, 4, 2, ROWS, DS), F32),
            pltpu.VMEM((2, 2, 4, 2, ROWS, DS), BF16),
            pltpu.VMEM((2, 2, 4, 2, ROWS, DS), BF16),
            pltpu.VMEM((2, 2, SLOTS, DS), BF16),
            pltpu.VMEM((2, 2, SLOTS, DS), BF16),
            pltpu.VMEM((7, PAD, DS), BF16),
            dma((8,)),
            dma((4,)),
            dma((3,)),
            dma((3,)),
            dma((3,)),
            dma((3, 2, 7)),
            dma((2,)),
            dma((2, 2, 7)),
            dma((2,)),
            dma((2,)),
        ],
        compiler_params=pltpu.CompilerParams(collective_id=0, has_side_effects=True),
    )(
        section_acts[0],
        section_input_gradients[0],
        saved_input[0],
        fwd_routes[0].T,
        fwd_probs[0].T,
        back_routes[0].T,
        back_probs[0].T,
        w_gate[0],
        w_up[0],
        w_down[0],
    )
    return out[None], out_grads[None]


def solution(mesh):
    spread = P("section", "expert", None)
    whole = P("section", None, None)
    return jax.shard_map(
        tick,
        mesh=mesh,
        in_specs=(spread, spread, spread, whole, whole, whole, whole, spread, spread, spread),
        out_specs=(spread, spread),
        check_vma=False,
    )
```

```python
import jax
import jax.numpy as jnp
from jax import lax
from jax.experimental import pallas as pl
from jax.experimental.pallas import tpu as pltpu
from jax.sharding import PartitionSpec as P

MESH = pl.DeviceIdType.MESH
BF16 = jnp.bfloat16
F32 = jnp.float32

TOP = 8
E_WIN = 4
Z = 8
Y = 8
TOK = 192
DS = 256
CAP = 12
PAD = 16
SLOTS = E_WIN * PAD
ROWS = E_WIN * CAP
HID = 128
HALF = Z * DS
X, G, B = 1, 2, 0
LONG, SHORT = 0, 4
DIRECT = (G,)


def dot_nt(a, b):
    return lax.dot_general(a, b, (((1,), (1,)), ((), ())), preferred_element_type=F32)


def dot_nn(a, b):
    return lax.dot_general(a, b, (((1,), (0,)), ((), ())), preferred_element_type=F32)


def dot_tn(a, b):
    return lax.dot_general(a, b, (((0,), (0,)), ((), ())), preferred_element_type=F32)


def own_tokens(whole, group):
    block = whole[:, 0:TOK]
    for g in range(1, E_WIN):
        block = jnp.where(group == g, whole[:, g * TOK : (g + 1) * TOK], block)
    return block


def pickers(routes, probs, group, before_ref):
    routes = own_tokens(routes, group)
    probs = own_tokens(probs, group)
    slot = lax.broadcasted_iota(jnp.int32, (SLOTS, TOK), 0)
    expert = slot // PAD
    chosen = jnp.zeros((SLOTS, TOK), F32)
    weight = jnp.zeros((SLOTS, TOK), F32)
    for e in range(E_WIN):
        hit = routes == e
        named = jnp.sum(jnp.where(hit, 1.0, 0.0), axis=0, keepdims=True)
        gain = jnp.sum(jnp.where(hit, probs, 0.0), axis=0, keepdims=True)
        chosen = jnp.where(expert == e, jnp.broadcast_to(named, (SLOTS, TOK)), chosen)
        weight = jnp.where(expert == e, jnp.broadcast_to(gain, (SLOTS, TOK)), weight)
    before = dot_nn(chosen.astype(BF16), before_ref[...])
    place = (slot - expert * PAD).astype(F32)
    mask = (before == place) & (chosen > 0.5)
    picker = jnp.where(mask, 1.0, 0.0).astype(BF16)
    column = jnp.sum(jnp.where(mask, weight, 0.0), axis=1, keepdims=True)
    return picker, column


def before_mask():
    t0 = lax.broadcasted_iota(jnp.int32, (TOK, TOK), 0)
    t1 = lax.broadcasted_iota(jnp.int32, (TOK, TOK), 1)
    return jnp.where(t0 < t1, 1.0, 0.0).astype(BF16)


def pack_matrix(shape, slot_axis):
    slot = lax.broadcasted_iota(jnp.int32, shape, slot_axis)
    row = lax.broadcasted_iota(jnp.int32, shape, 1 - slot_axis)
    same = row == (slot // PAD) * CAP + slot % PAD
    return jnp.where(same, jnp.where(slot % PAD < CAP, 1.0, 0.0), 0.0).astype(BF16)


def identity():
    i = lax.broadcasted_iota(jnp.int32, (SLOTS, SLOTS), 0)
    j = lax.broadcasted_iota(jnp.int32, (SLOTS, SLOTS), 1)
    return jnp.where(i == j, 1.0, 0.0).astype(BF16)


def kernel(
    acts,
    grads,
    saved,
    f_routes,
    f_probs,
    b_routes,
    b_probs,
    w_gate,
    w_up,
    w_down,
    out,
    out_grads,
    relay,
    kept,
    routes,
    probs,
    wgu,
    wd,
    earlier,
    pick,
    ex,
    rows,
    parts,
    ring_out,
    ring_in,
    fin,
    comb,
    meter,
    local_sem,
    relay_sem,
    small_send,
    ex_recv,
    ag_send,
    ag_recv,
    rs_send,
    rs_recv,
    fin_recv,
):
    me = lax.axis_index("expert")
    section = lax.axis_index("section")
    sections = lax.axis_size("section")
    y = me // Z
    z = me % Z
    g = y // 2
    r = y % 2
    up = y * Z + (z + 1) % Z
    down = y * Z + (z + Z - 1) % Z
    up_two = y * Z + (z + 2) % Z
    down_two = y * Z + (z + Z - 2) % Z
    after = (section + 1) % sections
    behind = (section + sections - 1) % sections
    columns = [((y + d) % Y) * Z + z for d in range(Y)]

    barrier = pltpu.get_barrier_semaphore()
    for d in (4, 3, 5, 2, 6, 1, 7):
        pl.semaphore_signal(barrier, inc=1, device_id={"expert": columns[d]}, device_id_type=MESH)
    for peer in (up, down, up_two, down_two):
        pl.semaphore_signal(barrier, inc=1, device_id={"expert": peer}, device_id_type=MESH)
    for peer in (after, behind):
        pl.semaphore_signal(barrier, inc=1, device_id={"section": peer}, device_id_type=MESH)

    loads = [
        pltpu.make_async_copy(b_routes, routes.at[1], local_sem.at[0]),
        pltpu.make_async_copy(b_probs, probs.at[1], local_sem.at[0]),
        pltpu.make_async_copy(saved, kept, local_sem.at[1]),
        pltpu.make_async_copy(f_routes, routes.at[0], local_sem.at[2]),
        pltpu.make_async_copy(f_probs, probs.at[0], local_sem.at[2]),
        pltpu.make_async_copy(w_gate, wgu.at[pl.ds(0, HID)], local_sem.at[3]),
        pltpu.make_async_copy(w_up, wgu.at[pl.ds(HID, HID)], local_sem.at[3]),
        pltpu.make_async_copy(w_down, wd, local_sem.at[4]),
    ]
    for load in loads:
        load.start()

    def expert_slots(e):
        return pl.ds(pl.multiple_of(e * PAD, PAD), PAD)

    def all_of(like, sem):
        pltpu.make_async_copy(like, like, sem).wait()


    def exchange(d):
        ex[d, r, expert_slots(g), :] = pick[d, expert_slots(g), :]
        for s in (4, 3, 5, 2, 6, 1, 7):
            pltpu.make_async_remote_copy(
                src_ref=pick.at[d, expert_slots(((y + s) % Y) // 2)],
                dst_ref=ex.at[d, r, expert_slots(g)],
                send_sem=small_send,
                recv_sem=ex_recv.at[d],
                device_id={"expert": columns[s]},
                device_id_type=MESH,
            ).start()

    def gather_own(d):
        all_of(meter.at[0], ex_recv.at[d])
        for half in range(2):
            rows[d, z, half] = dot_nn(packer, ex[d, half]).astype(BF16)
        pass_on(d, 0, LONG)
        pass_on(d, 0, SHORT)
        absorb(d, ((z, 0), (z, 1)))

    ag_copies = {}

    def pass_on(d, hop, chain):
        for way in range(2):
            half = way if chain == LONG else 1 - way
            block = (z + Z - hop) % Z if way == 0 else (z + hop) % Z
            piece = rows.at[d, block, half]
            copy = pltpu.make_async_remote_copy(
                src_ref=piece,
                dst_ref=piece,
                send_sem=ag_send,
                recv_sem=ag_recv.at[d, way, chain + hop],
                device_id={"expert": up if way == 0 else down},
                device_id_type=MESH,
            )
            if hop > 0:
                ag_copies[d, way, hop - 1, chain].wait_recv()
            if hop == 2 and chain == LONG and d in DIRECT:
                skip(d, way)
            ag_copies[d, way, hop, chain] = copy
            copy.start()

    def skip(d, way):
        block = (z + Z - 2) % Z if way == 0 else (z + 2) % Z
        piece = rows.at[d, block, way]
        copy = pltpu.make_async_remote_copy(
            src_ref=piece,
            dst_ref=piece,
            send_sem=ag_send,
            recv_sem=ag_recv.at[d, way, LONG + 3],
            device_id={"expert": up_two if way == 0 else down_two},
            device_id_type=MESH,
        )
        ag_copies[d, way, 3, LONG] = copy
        copy.start()

    def features(block, half):
        return pl.ds(pl.multiple_of(half * HALF + block * DS, DS), DS)

    totals = {B: None, X: None, G: None}

    def absorb(d, blocks):
        for block, half in blocks:
            weights = wd if d == G else wgu
            term = dot_nt(rows[d, block, half], weights[:, features(block, half)])
            totals[d] = term if totals[d] is None else totals[d] + term

    def arrived(d, hop, chain):
        if hop < 2 or (hop == 2 and chain == LONG and d not in DIRECT):
            pass_on(d, hop + 1, chain)
        else:
            for way in range(2):
                ag_copies[d, way, hop, chain].wait_recv()
        first, second = (0, 1) if chain == LONG else (1, 0)
        absorb(d, (((z + Z - hop - 1) % Z, first), ((z + hop + 1) % Z, second)))

    pl.semaphore_wait(barrier, 13)

    relays = [
        pltpu.make_async_remote_copy(
            src_ref=source,
            dst_ref=relay.at[i],
            send_sem=relay_sem.at[i],
            recv_sem=relay_sem.at[2 + i],
            device_id={"section": peer},
            device_id_type=MESH,
        )
        for i, (source, peer) in enumerate(((acts, after), (grads, behind)))
    ]
    for copy in relays:
        copy.start()

    earlier[...] = before_mask()
    all_of(probs, local_sem.at[0])
    b_picker, b_column = pickers(routes[1], probs[1], g, earlier)
    loads[2].wait()
    pick[B] = dot_nn(b_picker, kept[...]).astype(BF16)
    exchange(B)
    all_of(probs, local_sem.at[2])
    f_picker, f_column = pickers(routes[0], probs[0], g, earlier)

    relays[0].wait_recv()
    pick[X] = dot_nn(f_picker, relay[0]).astype(BF16)
    exchange(X)
    relays[1].wait_recv()
    pick[G] = (dot_nn(b_picker, relay[1]) * b_column).astype(BF16)
    exchange(G)

    packer = pack_matrix((ROWS, SLOTS), 1)
    unpacker = pack_matrix((SLOTS, ROWS), 0)
    token_of = [dot_tn(p, identity()).astype(BF16) for p in (f_picker, b_picker)]

    all_of(wgu, local_sem.at[3])
    all_of(wd, local_sem.at[4])

    gather_own(B)
    gather_own(X)
    arrived(B, 0, LONG)
    arrived(B, 0, SHORT)
    gather_own(G)
    for d, hop in ((X, 0), (B, 1), (G, 0), (X, 1), (B, 2), (G, 1), (X, 2)):
        arrived(d, hop, LONG)
        arrived(d, hop, SHORT)
    arrived(B, 3, LONG)
    arrived(G, 2, LONG)
    arrived(G, 2, SHORT)

    rs_copies = {}

    def own_part(c, block, half):
        if c == 0:
            return dot_nn(made[0], wd[:, features(block, half)])
        return dot_nn(made[1], wgu[:, features(block, half)])

    def turns(turn):
        if turn == 0:
            for way in range(2):
                yield way, way, 0
        for far in (0, 1):
            for way in range(2):
                yield way, way if far else 1 - way, turn + 1

    def part_of(way, step):
        return (z + 4 - step) % Z if way == 0 else (z + 4 + step) % Z

    def own_parts(c, turn):
        for way, half, step in turns(turn):
            parts[c, way, step, half] = own_part(c, part_of(way, step), half)

    def reduce_turn(c, turn):
        for way, half, step in turns(turn):
            value = parts[c, way, step, half] if turn > 0 else own_part(c, part_of(way, step), half)
            sources = (1, 0) if step == 2 and half == way else (step - 1,) if step > 1 else ()
            for source in sources:
                rs_copies[c, way, half, source].wait_recv()
                value = value + ring_in[c, way, source, half].astype(F32)
            ring_out[c, way, step, half] = value.astype(BF16)
            at = (c, way, step, half)
            next_one, next_two = (up, up_two) if way == 0 else (down, down_two)
            copy = pltpu.make_async_remote_copy(
                src_ref=ring_out.at[at],
                dst_ref=ring_in.at[at],
                send_sem=rs_send,
                recv_sem=rs_recv.at[c, way, step if half == way else 3 + step],
                device_id={"expert": next_two if step == 0 else next_one},
                device_id_type=MESH,
            )
            rs_copies[c, way, half, step] = copy
            copy.start()

    def send_back(c):
        mine = [own_part(c, z, half) for half in range(2)]
        for half in range(2):
            value = mine[half]
            for way in (1 - half, half):
                rs_copies[c, way, half, 3].wait_recv()
                value = value + ring_in[c, way, 3, half].astype(F32)
            fin[c, half] = dot_nn(unpacker, value.astype(BF16)).astype(BF16)
        comb[c, r, expert_slots(g), :] = fin[c, r, expert_slots(g), :]
        for s in (4, 3, 5, 2, 6, 1, 7):
            to = (y + s) % Y
            pltpu.make_async_remote_copy(
                src_ref=fin.at[c, to % 2, expert_slots(to // 2)],
                dst_ref=comb.at[c, r, expert_slots(g)],
                send_sem=small_send,
                recv_sem=fin_recv.at[c],
                device_id={"expert": columns[s]},
                device_id_type=MESH,
            ).start()

    def place(picker, values):
        high = values.astype(BF16)
        low = (values - high.astype(F32)).astype(BF16)
        return dot_nn(picker, high) + dot_nn(picker, low)

    def finish(c, picker, column, base, target):
        all_of(meter.at[0], fin_recv.at[c])
        values = comb[c, 0].astype(F32) + comb[c, 1].astype(F32)
        if column is not None:
            values = values * column
        target[...] = (base.astype(F32) + place(picker, values)).astype(BF16)

    made = {}

    arrived(X, 3, LONG)
    gate, upper = totals[X][:, :HID], totals[X][:, HID:]
    made[0] = (gate * jax.nn.sigmoid(gate) * upper).astype(BF16)
    reduce_turn(0, 0)

    gate, upper = totals[B][:, :HID], totals[B][:, HID:]
    sig = jax.nn.sigmoid(gate)
    act = gate * sig
    slope = upper * sig * (1.0 + gate * (1.0 - sig))
    arrived(G, 3, LONG)
    d_hidden = totals[G]
    made[1] = jnp.concatenate([(d_hidden * slope).astype(BF16), (d_hidden * act).astype(BF16)], axis=1)
    reduce_turn(1, 0)
    for turn in range(1, 3):
        for c in range(2):
            own_parts(c, turn)
            reduce_turn(c, turn)
    send_back(0)
    send_back(1)
    finish(0, token_of[0], f_column, relay[0], out)
    finish(1, token_of[1], None, relay[1], out_grads)

    def drain():
        for copy in relays:
            copy.wait_send()
        all_of(meter, small_send)
        all_of(rows.at[:, pl.ds(0, 7)], ag_send)
        all_of(rows.at[pl.ds(0, 2), pl.ds(0, 7)], rs_send)

    drain()


def write_out(first, second, out, out_grads, sem):
    copies = [pltpu.make_async_copy(a, b, sem.at[i]) for i, (a, b) in enumerate(((first, out), (second, out_grads)))]
    for copy in copies:
        copy.start()
    for copy in copies:
        copy.wait()


def tick(section_acts, section_input_gradients, saved_input, fwd_routes, fwd_probs, back_routes, back_probs, w_gate, w_up, w_down):
    anywhere = pl.BlockSpec(memory_space=pl.ANY)
    inside = pl.BlockSpec(memory_space=pltpu.VMEM)
    block = pltpu.VMEM((TOK, DS), BF16)
    dma = pltpu.SemaphoreType.DMA
    out, out_grads = pl.pallas_call(
        kernel,
        out_shape=(block, block),
        in_specs=[anywhere] * 10,
        out_specs=(inside, inside),
        scratch_shapes=[
            pltpu.VMEM((2, TOK, DS), BF16),
            pltpu.VMEM((TOK, DS), BF16),
            pltpu.VMEM((2, TOP, E_WIN * TOK), jnp.int32),
            pltpu.VMEM((2, TOP, E_WIN * TOK), F32),
            pltpu.VMEM((2 * HID, 2 * HALF), BF16),
            pltpu.VMEM((HID, 2 * HALF), BF16),
            pltpu.VMEM((TOK, TOK), BF16),
            pltpu.VMEM((3, SLOTS, DS), BF16),
            pltpu.VMEM((3, 2, SLOTS, DS), BF16),
            pltpu.VMEM((3, Z, 2, ROWS, DS), BF16),
            pltpu.VMEM((2, 2, 4, 2, ROWS, DS), F32),
            pltpu.VMEM((2, 2, 4, 2, ROWS, DS), BF16),
            pltpu.VMEM((2, 2, 4, 2, ROWS, DS), BF16),
            pltpu.VMEM((2, 2, SLOTS, DS), BF16),
            pltpu.VMEM((2, 2, SLOTS, DS), BF16),
            pltpu.VMEM((5, 7, PAD, DS), BF16),
            dma((5,)),
            dma((4,)),
            dma,
            dma((3,)),
            dma,
            dma((3, 2, 7)),
            dma,
            dma((2, 2, 7)),
            dma((2,)),
        ],
        compiler_params=pltpu.CompilerParams(collective_id=0, has_side_effects=True),
    )(
        section_acts[0],
        section_input_gradients[0],
        saved_input[0],
        fwd_routes[0].T,
        fwd_probs[0].T,
        back_routes[0].T,
        back_probs[0].T,
        w_gate[0],
        w_up[0],
        w_down[0],
    )
    block = jax.ShapeDtypeStruct((TOK, DS), BF16)
    out, out_grads = pl.pallas_call(
        write_out,
        out_shape=(block, block),
        in_specs=[inside] * 2,
        out_specs=(anywhere, anywhere),
        scratch_shapes=[dma((2,))],
    )(*(pltpu.with_memory_space_constraint(v, pltpu.VMEM) for v in (out, out_grads)))
    return out[None], out_grads[None]


def solution(mesh):
    spread = P("section", "expert", None)
    whole = P("section", None, None)
    return jax.shard_map(
        tick,
        mesh=mesh,
        in_specs=(spread, spread, spread, whole, whole, whole, whole, spread, spread, spread),
        out_specs=(spread, spread),
        check_vma=False,
    )
```

```python
import jax
import jax.numpy as jnp
from jax import lax
from jax.experimental import pallas as pl
from jax.experimental.pallas import tpu as pltpu
from jax.sharding import PartitionSpec as P

MESH = pl.DeviceIdType.MESH
BF16 = jnp.bfloat16
F32 = jnp.float32

TOP = 8
E_WIN = 4
Z = 8
Y = 8
TOK = 192
DS = 256
CAP = 12
PAD = 16
SLOTS = E_WIN * PAD
ROWS = E_WIN * CAP
HID = 128
HALF = Z * DS
X, G, B = 1, 2, 0
LONG, SHORT = 0, 4
DIRECT = (G,)


def dot_nt(a, b):
    return lax.dot_general(a, b, (((1,), (1,)), ((), ())), preferred_element_type=F32)


def dot_nn(a, b):
    return lax.dot_general(a, b, (((1,), (0,)), ((), ())), preferred_element_type=F32)


def dot_tn(a, b):
    return lax.dot_general(a, b, (((0,), (0,)), ((), ())), preferred_element_type=F32)


def own_tokens(whole, group):
    block = whole[:, 0:TOK]
    for g in range(1, E_WIN):
        block = jnp.where(group == g, whole[:, g * TOK : (g + 1) * TOK], block)
    return block


def pickers(routes, probs, group, before_ref):
    routes = own_tokens(routes, group)
    probs = own_tokens(probs, group)
    slot = lax.broadcasted_iota(jnp.int32, (SLOTS, TOK), 0)
    expert = slot // PAD
    chosen = jnp.zeros((SLOTS, TOK), F32)
    weight = jnp.zeros((SLOTS, TOK), F32)
    for e in range(E_WIN):
        hit = routes == e
        named = jnp.sum(jnp.where(hit, 1.0, 0.0), axis=0, keepdims=True)
        gain = jnp.sum(jnp.where(hit, probs, 0.0), axis=0, keepdims=True)
        chosen = jnp.where(expert == e, jnp.broadcast_to(named, (SLOTS, TOK)), chosen)
        weight = jnp.where(expert == e, jnp.broadcast_to(gain, (SLOTS, TOK)), weight)
    before = dot_nn(chosen.astype(BF16), before_ref[...])
    place = (slot - expert * PAD).astype(F32)
    mask = (before == place) & (chosen > 0.5)
    picker = jnp.where(mask, 1.0, 0.0).astype(BF16)
    column = jnp.sum(jnp.where(mask, weight, 0.0), axis=1, keepdims=True)
    return picker, column


def before_mask():
    t0 = lax.broadcasted_iota(jnp.int32, (TOK, TOK), 0)
    t1 = lax.broadcasted_iota(jnp.int32, (TOK, TOK), 1)
    return jnp.where(t0 < t1, 1.0, 0.0).astype(BF16)


def pack_matrix(shape, slot_axis):
    slot = lax.broadcasted_iota(jnp.int32, shape, slot_axis)
    row = lax.broadcasted_iota(jnp.int32, shape, 1 - slot_axis)
    same = row == (slot // PAD) * CAP + slot % PAD
    return jnp.where(same, jnp.where(slot % PAD < CAP, 1.0, 0.0), 0.0).astype(BF16)


def identity():
    i = lax.broadcasted_iota(jnp.int32, (SLOTS, SLOTS), 0)
    j = lax.broadcasted_iota(jnp.int32, (SLOTS, SLOTS), 1)
    return jnp.where(i == j, 1.0, 0.0).astype(BF16)


def kernel(
    acts,
    grads,
    saved,
    f_routes,
    f_probs,
    b_routes,
    b_probs,
    w_gate,
    w_up,
    w_down,
    out,
    out_grads,
    relay,
    kept,
    routes,
    probs,
    wgu,
    wd,
    earlier,
    pick,
    ex,
    rows,
    parts,
    ring_out,
    ring_in,
    fin,
    comb,
    meter,
    local_sem,
    relay_sem,
    small_send,
    ex_recv,
    ag_send,
    ag_recv,
    rs_send,
    rs_recv,
    fin_recv,
):
    me = lax.axis_index("expert")
    section = lax.axis_index("section")
    sections = lax.axis_size("section")
    y = me // Z
    z = me % Z
    g = y // 2
    r = y % 2
    up = y * Z + (z + 1) % Z
    down = y * Z + (z + Z - 1) % Z
    partner = (2 * g + 1 - r) * Z + z
    up_two = y * Z + (z + 2) % Z
    down_two = y * Z + (z + Z - 2) % Z
    after = (section + 1) % sections
    behind = (section + sections - 1) % sections
    columns = [((y + d) % Y) * Z + z for d in range(Y)]

    barrier = pltpu.get_barrier_semaphore()
    for d in (4, 3, 5, 2, 6, 1, 7):
        pl.semaphore_signal(barrier, inc=1, device_id={"expert": columns[d]}, device_id_type=MESH)
    for peer in (up, down, up_two, down_two):
        pl.semaphore_signal(barrier, inc=1, device_id={"expert": peer}, device_id_type=MESH)
    for peer in (after, behind):
        pl.semaphore_signal(barrier, inc=1, device_id={"section": peer}, device_id_type=MESH)

    loads = [
        pltpu.make_async_copy(b_routes, routes.at[1], local_sem.at[0]),
        pltpu.make_async_copy(b_probs, probs.at[1], local_sem.at[0]),
        pltpu.make_async_copy(saved, kept, local_sem.at[1]),
        pltpu.make_async_copy(f_routes, routes.at[0], local_sem.at[2]),
        pltpu.make_async_copy(f_probs, probs.at[0], local_sem.at[2]),
        pltpu.make_async_copy(w_gate, wgu.at[pl.ds(0, HID)], local_sem.at[3]),
        pltpu.make_async_copy(w_up, wgu.at[pl.ds(HID, HID)], local_sem.at[3]),
        pltpu.make_async_copy(w_down, wd, local_sem.at[4]),
    ]
    for load in loads:
        load.start()

    def expert_slots(e):
        return pl.ds(pl.multiple_of(e * PAD, PAD), PAD)

    def all_of(like, sem):
        pltpu.make_async_copy(like, like, sem).wait()


    def exchange(d):
        ex[d, r, expert_slots(g), :] = pick[d, expert_slots(g), :]
        for s in (4, 3, 5, 2, 6, 1, 7):
            pltpu.make_async_remote_copy(
                src_ref=pick.at[d, expert_slots(((y + s) % Y) // 2)],
                dst_ref=ex.at[d, r, expert_slots(g)],
                send_sem=small_send,
                recv_sem=ex_recv.at[d],
                device_id={"expert": columns[s]},
                device_id_type=MESH,
            ).start()

    def gather_own(d):
        all_of(meter.at[0], ex_recv.at[d])
        for half in range(2):
            rows[d, z, half] = dot_nn(packer, ex[d, half]).astype(BF16)
        if d == B:
            own_hop(0)
            other_hop(0)
        else:
            pass_on(d, 0, LONG)
            pass_on(d, 0, SHORT)
        absorb(d, ((z, 0), (z, 1)))

    ag_copies = {}
    paired = {}

    def send_piece(key, block, half, peer, sem):
        piece = rows.at[B, block, half]
        paired[key] = pltpu.make_async_remote_copy(
            src_ref=piece,
            dst_ref=piece,
            send_sem=ag_send,
            recv_sem=ag_recv.at[B, sem // 7, sem % 7],
            device_id={"expert": peer},
            device_id_type=MESH,
        )
        paired[key].start()

    def beside(way, distance):
        return (z + Z - distance) % Z if way == 0 else (z + distance) % Z

    def own_hop(hop):
        for way in range(2):
            if hop > 0:
                paired["own", way, hop - 1].wait_recv()
            if hop < 3:
                send_piece(("own", way, hop), beside(way, hop), r, up if way == 0 else down, way * 3 + hop)
            else:
                send_piece(("pair", way), beside(way, 3), r, partner, 10 + way)
        if hop == 3:
            send_piece("far", (z + 5 + 6 * r) % Z, r, up + r * (down - up), 12)

    def other_hop(hop):
        for way in range(2):
            if hop > 0:
                paired["other", way, hop - 1].wait_recv()
            if hop < 2:
                send_piece(("other", way, hop), beside(way, hop), 1 - r, up if way == 0 else down, 6 + way * 2 + hop)

    def arrived_kept(hop, chain):
        if chain == LONG and hop < 3:
            own_hop(hop + 1)
            absorb(B, [(beside(way, hop + 1), r) for way in range(2)])
        elif chain == LONG:
            paired["far"].wait_recv()
            send_piece("last", (z + 4) % Z, r, partner, 13)
            absorb(B, [((z + 4) % Z, r)])
        elif hop < 2:
            other_hop(hop + 1)
            absorb(B, [(beside(way, hop + 1), 1 - r) for way in range(2)])

    def arrived_pair():
        for way in range(2):
            paired["pair", way].wait_recv()
        absorb(B, [(beside(way, 3), 1 - r) for way in range(2)])
        paired["last"].wait_recv()
        absorb(B, [((z + 4) % Z, 1 - r)])

    def pass_on(d, hop, chain):
        for way in range(2):
            half = way if chain == LONG else 1 - way
            block = (z + Z - hop) % Z if way == 0 else (z + hop) % Z
            piece = rows.at[d, block, half]
            copy = pltpu.make_async_remote_copy(
                src_ref=piece,
                dst_ref=piece,
                send_sem=ag_send,
                recv_sem=ag_recv.at[d, way, chain + hop],
                device_id={"expert": up if way == 0 else down},
                device_id_type=MESH,
            )
            if hop > 0:
                ag_copies[d, way, hop - 1, chain].wait_recv()
            if hop == 2 and chain == LONG and d in DIRECT:
                skip(d, way)
            ag_copies[d, way, hop, chain] = copy
            copy.start()

    def skip(d, way):
        block = (z + Z - 2) % Z if way == 0 else (z + 2) % Z
        piece = rows.at[d, block, way]
        copy = pltpu.make_async_remote_copy(
            src_ref=piece,
            dst_ref=piece,
            send_sem=ag_send,
            recv_sem=ag_recv.at[d, way, LONG + 3],
            device_id={"expert": up_two if way == 0 else down_two},
            device_id_type=MESH,
        )
        ag_copies[d, way, 3, LONG] = copy
        copy.start()

    def features(block, half):
        return pl.ds(pl.multiple_of(half * HALF + block * DS, DS), DS)

    totals = {B: None, X: None, G: None}

    def absorb(d, blocks):
        for block, half in blocks:
            weights = wd if d == G else wgu
            term = dot_nt(rows[d, block, half], weights[:, features(block, half)])
            totals[d] = term if totals[d] is None else totals[d] + term

    def arrived(d, hop, chain):
        if d == B:
            arrived_kept(hop, chain)
            return
        if hop < 2 or (hop == 2 and chain == LONG and d not in DIRECT):
            pass_on(d, hop + 1, chain)
        else:
            for way in range(2):
                ag_copies[d, way, hop, chain].wait_recv()
        first, second = (0, 1) if chain == LONG else (1, 0)
        absorb(d, (((z + Z - hop - 1) % Z, first), ((z + hop + 1) % Z, second)))

    earlier[...] = before_mask()
    all_of(probs, local_sem.at[0])
    b_picker, b_column = pickers(routes[1], probs[1], g, earlier)
    loads[2].wait()
    pick[B] = dot_nn(b_picker, kept[...]).astype(BF16)
    pl.semaphore_wait(barrier, 13)

    relays = [
        pltpu.make_async_remote_copy(
            src_ref=source,
            dst_ref=relay.at[i],
            send_sem=relay_sem.at[i],
            recv_sem=relay_sem.at[2 + i],
            device_id={"section": peer},
            device_id_type=MESH,
        )
        for i, (source, peer) in enumerate(((acts, after), (grads, behind)))
    ]
    for copy in relays:
        copy.start()

    exchange(B)
    all_of(probs, local_sem.at[2])
    f_picker, f_column = pickers(routes[0], probs[0], g, earlier)

    relays[0].wait_recv()
    pick[X] = dot_nn(f_picker, relay[0]).astype(BF16)
    exchange(X)
    relays[1].wait_recv()
    pick[G] = (dot_nn(b_picker, relay[1]) * b_column).astype(BF16)
    exchange(G)

    packer = pack_matrix((ROWS, SLOTS), 1)
    unpacker = pack_matrix((SLOTS, ROWS), 0)
    token_of = [dot_tn(p, identity()).astype(BF16) for p in (f_picker, b_picker)]

    all_of(wgu, local_sem.at[3])
    all_of(wd, local_sem.at[4])

    gather_own(B)
    gather_own(X)
    arrived(B, 0, LONG)
    arrived(B, 0, SHORT)
    gather_own(G)
    for d, hop in ((X, 0), (B, 1), (G, 0), (X, 1), (B, 2), (G, 1), (X, 2)):
        arrived(d, hop, LONG)
        arrived(d, hop, SHORT)
    arrived(B, 3, LONG)
    arrived(G, 2, LONG)
    arrived(G, 2, SHORT)
    arrived_pair()

    rs_copies = {}

    def own_part(c, block, half):
        if c == 0:
            return dot_nn(made[0], wd[:, features(block, half)])
        return dot_nn(made[1], wgu[:, features(block, half)])

    def turns(turn):
        if turn == 0:
            for way in range(2):
                yield way, way, 0
        for far in (0, 1):
            for way in range(2):
                yield way, way if far else 1 - way, turn + 1

    def part_of(way, step):
        return (z + 4 - step) % Z if way == 0 else (z + 4 + step) % Z

    def own_parts(c, turn):
        for way, half, step in turns(turn):
            parts[c, way, step, half] = own_part(c, part_of(way, step), half)

    def reduce_turn(c, turn):
        for way, half, step in turns(turn):
            value = parts[c, way, step, half] if turn > 0 else own_part(c, part_of(way, step), half)
            sources = (1, 0) if step == 2 and half == way else (step - 1,) if step > 1 else ()
            for source in sources:
                rs_copies[c, way, half, source].wait_recv()
                value = value + ring_in[c, way, source, half].astype(F32)
            ring_out[c, way, step, half] = value.astype(BF16)
            at = (c, way, step, half)
            next_one, next_two = (up, up_two) if way == 0 else (down, down_two)
            copy = pltpu.make_async_remote_copy(
                src_ref=ring_out.at[at],
                dst_ref=ring_in.at[at],
                send_sem=rs_send,
                recv_sem=rs_recv.at[c, way, step if half == way else 3 + step],
                device_id={"expert": next_two if step == 0 else next_one},
                device_id_type=MESH,
            )
            rs_copies[c, way, half, step] = copy
            copy.start()

    def send_back(c):
        mine = [own_part(c, z, half) for half in range(2)]
        for half in range(2):
            value = mine[half]
            for way in (1 - half, half):
                rs_copies[c, way, half, 3].wait_recv()
                value = value + ring_in[c, way, 3, half].astype(F32)
            fin[c, half] = dot_nn(unpacker, value.astype(BF16)).astype(BF16)
        comb[c, r, expert_slots(g), :] = fin[c, r, expert_slots(g), :]
        for s in (4, 3, 5, 2, 6, 1, 7):
            to = (y + s) % Y
            pltpu.make_async_remote_copy(
                src_ref=fin.at[c, to % 2, expert_slots(to // 2)],
                dst_ref=comb.at[c, r, expert_slots(g)],
                send_sem=small_send,
                recv_sem=fin_recv.at[c],
                device_id={"expert": columns[s]},
                device_id_type=MESH,
            ).start()

    def place(picker, values):
        high = values.astype(BF16)
        low = (values - high.astype(F32)).astype(BF16)
        return dot_nn(picker, high) + dot_nn(picker, low)

    def finish(c, picker, column, base, target):
        all_of(meter.at[0], fin_recv.at[c])
        values = comb[c, 0].astype(F32) + comb[c, 1].astype(F32)
        if column is not None:
            values = values * column
        target[...] = (base.astype(F32) + place(picker, values)).astype(BF16)

    made = {}

    arrived(X, 3, LONG)
    gate, upper = totals[X][:, :HID], totals[X][:, HID:]
    made[0] = (gate * jax.nn.sigmoid(gate) * upper).astype(BF16)
    reduce_turn(0, 0)

    gate, upper = totals[B][:, :HID], totals[B][:, HID:]
    sig = jax.nn.sigmoid(gate)
    act = gate * sig
    slope = upper * sig * (1.0 + gate * (1.0 - sig))
    arrived(G, 3, LONG)
    d_hidden = totals[G]
    made[1] = jnp.concatenate([(d_hidden * slope).astype(BF16), (d_hidden * act).astype(BF16)], axis=1)
    reduce_turn(1, 0)
    for turn in range(1, 3):
        for c in range(2):
            own_parts(c, turn)
            reduce_turn(c, turn)
    send_back(0)
    send_back(1)
    finish(0, token_of[0], f_column, relay[0], out)
    finish(1, token_of[1], None, relay[1], out_grads)

    def drain():
        for copy in relays:
            copy.wait_send()
        all_of(meter, small_send)
        all_of(rows.at[:, pl.ds(0, 7)], ag_send)
        all_of(rows.at[pl.ds(0, 2), pl.ds(0, 7)], rs_send)

    drain()


def write_out(first, second, out, out_grads, sem):
    copies = [pltpu.make_async_copy(a, b, sem.at[i]) for i, (a, b) in enumerate(((first, out), (second, out_grads)))]
    for copy in copies:
        copy.start()
    for copy in copies:
        copy.wait()


def tick(section_acts, section_input_gradients, saved_input, fwd_routes, fwd_probs, back_routes, back_probs, w_gate, w_up, w_down):
    anywhere = pl.BlockSpec(memory_space=pl.ANY)
    inside = pl.BlockSpec(memory_space=pltpu.VMEM)
    block = pltpu.VMEM((TOK, DS), BF16)
    dma = pltpu.SemaphoreType.DMA
    out, out_grads = pl.pallas_call(
        kernel,
        out_shape=(block, block),
        in_specs=[anywhere] * 10,
        out_specs=(inside, inside),
        scratch_shapes=[
            pltpu.VMEM((2, TOK, DS), BF16),
            pltpu.VMEM((TOK, DS), BF16),
            pltpu.VMEM((2, TOP, E_WIN * TOK), jnp.int32),
            pltpu.VMEM((2, TOP, E_WIN * TOK), F32),
            pltpu.VMEM((2 * HID, 2 * HALF), BF16),
            pltpu.VMEM((HID, 2 * HALF), BF16),
            pltpu.VMEM((TOK, TOK), BF16),
            pltpu.VMEM((3, SLOTS, DS), BF16),
            pltpu.VMEM((3, 2, SLOTS, DS), BF16),
            pltpu.VMEM((3, Z, 2, ROWS, DS), BF16),
            pltpu.VMEM((2, 2, 4, 2, ROWS, DS), F32),
            pltpu.VMEM((2, 2, 4, 2, ROWS, DS), BF16),
            pltpu.VMEM((2, 2, 4, 2, ROWS, DS), BF16),
            pltpu.VMEM((2, 2, SLOTS, DS), BF16),
            pltpu.VMEM((2, 2, SLOTS, DS), BF16),
            pltpu.VMEM((5, 7, PAD, DS), BF16),
            dma((5,)),
            dma((4,)),
            dma,
            dma((3,)),
            dma,
            dma((3, 2, 7)),
            dma,
            dma((2, 2, 7)),
            dma((2,)),
        ],
        compiler_params=pltpu.CompilerParams(collective_id=0, has_side_effects=True),
    )(
        section_acts[0],
        section_input_gradients[0],
        saved_input[0],
        fwd_routes[0].T,
        fwd_probs[0].T,
        back_routes[0].T,
        back_probs[0].T,
        w_gate[0],
        w_up[0],
        w_down[0],
    )
    block = jax.ShapeDtypeStruct((TOK, DS), BF16)
    out, out_grads = pl.pallas_call(
        write_out,
        out_shape=(block, block),
        in_specs=[inside] * 2,
        out_specs=(anywhere, anywhere),
        scratch_shapes=[dma((2,))],
    )(*(pltpu.with_memory_space_constraint(v, pltpu.VMEM) for v in (out, out_grads)))
    return out[None], out_grads[None]


def solution(mesh):
    spread = P("section", "expert", None)
    whole = P("section", None, None)
    return jax.shard_map(
        tick,
        mesh=mesh,
        in_specs=(spread, spread, spread, whole, whole, whole, whole, spread, spread, spread),
        out_specs=(spread, spread),
        check_vma=False,
    )
```

```python
import jax
import jax.numpy as jnp
from jax import lax
from jax.experimental import pallas as pl
from jax.experimental.pallas import tpu as pltpu
from jax.sharding import PartitionSpec as P

MESH = pl.DeviceIdType.MESH
BF16 = jnp.bfloat16
F32 = jnp.float32

TOP = 8
E_WIN = 4
Z = 8
Y = 8
TOK = 192
DS = 256
CAP = 12
PAD = 16
SLOTS = E_WIN * PAD
ROWS = E_WIN * CAP
HID = 128
HALF = Z * DS
X, G, B = 1, 2, 0
LONG, SHORT = 0, 4
DIRECT = (G,)


def dot_nt(a, b):
    return lax.dot_general(a, b, (((1,), (1,)), ((), ())), preferred_element_type=F32)


def dot_nn(a, b):
    return lax.dot_general(a, b, (((1,), (0,)), ((), ())), preferred_element_type=F32)


def dot_tn(a, b):
    return lax.dot_general(a, b, (((0,), (0,)), ((), ())), preferred_element_type=F32)


def own_tokens(whole, group):
    block = whole[:, 0:TOK]
    for g in range(1, E_WIN):
        block = jnp.where(group == g, whole[:, g * TOK : (g + 1) * TOK], block)
    return block


def pickers(routes, probs, group, before_ref):
    routes = own_tokens(routes, group)
    probs = own_tokens(probs, group)
    slot = lax.broadcasted_iota(jnp.int32, (SLOTS, TOK), 0)
    expert = slot // PAD
    chosen = jnp.zeros((SLOTS, TOK), F32)
    weight = jnp.zeros((SLOTS, TOK), F32)
    for e in range(E_WIN):
        hit = routes == e
        named = jnp.sum(jnp.where(hit, 1.0, 0.0), axis=0, keepdims=True)
        gain = jnp.sum(jnp.where(hit, probs, 0.0), axis=0, keepdims=True)
        chosen = jnp.where(expert == e, jnp.broadcast_to(named, (SLOTS, TOK)), chosen)
        weight = jnp.where(expert == e, jnp.broadcast_to(gain, (SLOTS, TOK)), weight)
    before = dot_nn(chosen.astype(BF16), before_ref[...])
    place = (slot - expert * PAD).astype(F32)
    mask = (before == place) & (chosen > 0.5)
    picker = jnp.where(mask, 1.0, 0.0).astype(BF16)
    column = jnp.sum(jnp.where(mask, weight, 0.0), axis=1, keepdims=True)
    return picker, column


def before_mask():
    t0 = lax.broadcasted_iota(jnp.int32, (TOK, TOK), 0)
    t1 = lax.broadcasted_iota(jnp.int32, (TOK, TOK), 1)
    return jnp.where(t0 < t1, 1.0, 0.0).astype(BF16)


def pack_matrix(shape, slot_axis):
    slot = lax.broadcasted_iota(jnp.int32, shape, slot_axis)
    row = lax.broadcasted_iota(jnp.int32, shape, 1 - slot_axis)
    same = row == (slot // PAD) * CAP + slot % PAD
    return jnp.where(same, jnp.where(slot % PAD < CAP, 1.0, 0.0), 0.0).astype(BF16)


def identity():
    i = lax.broadcasted_iota(jnp.int32, (SLOTS, SLOTS), 0)
    j = lax.broadcasted_iota(jnp.int32, (SLOTS, SLOTS), 1)
    return jnp.where(i == j, 1.0, 0.0).astype(BF16)


def kernel(
    acts,
    grads,
    saved,
    f_routes,
    f_probs,
    b_routes,
    b_probs,
    w_gate,
    w_up,
    w_down,
    out,
    out_grads,
    relay,
    kept,
    routes,
    probs,
    wgu,
    wd,
    earlier,
    pick,
    ex,
    rows,
    parts,
    ring_out,
    ring_in,
    fin,
    comb,
    meter,
    local_sem,
    relay_sem,
    small_send,
    ex_recv,
    ag_send,
    ag_recv,
    rs_send,
    rs_recv,
    fin_recv,
):
    me = lax.axis_index("expert")
    section = lax.axis_index("section")
    sections = lax.axis_size("section")
    y = me // Z
    z = me % Z
    g = y // 2
    r = y % 2
    up = y * Z + (z + 1) % Z
    down = y * Z + (z + Z - 1) % Z
    partner = (2 * g + 1 - r) * Z + z
    up_two = y * Z + (z + 2) % Z
    down_two = y * Z + (z + Z - 2) % Z
    after = (section + 1) % sections
    behind = (section + sections - 1) % sections
    columns = [((y + d) % Y) * Z + z for d in range(Y)]

    barrier = pltpu.get_barrier_semaphore()
    for d in (4, 3, 5, 2, 6, 1, 7):
        pl.semaphore_signal(barrier, inc=1, device_id={"expert": columns[d]}, device_id_type=MESH)
    for peer in (up, down, up_two, down_two):
        pl.semaphore_signal(barrier, inc=1, device_id={"expert": peer}, device_id_type=MESH)
    for peer in (after, behind):
        pl.semaphore_signal(barrier, inc=1, device_id={"section": peer}, device_id_type=MESH)

    loads = [
        pltpu.make_async_copy(b_routes, routes.at[1], local_sem.at[0]),
        pltpu.make_async_copy(b_probs, probs.at[1], local_sem.at[0]),
        pltpu.make_async_copy(saved, kept, local_sem.at[1]),
        pltpu.make_async_copy(f_routes, routes.at[0], local_sem.at[2]),
        pltpu.make_async_copy(f_probs, probs.at[0], local_sem.at[2]),
        pltpu.make_async_copy(w_gate, wgu.at[pl.ds(0, HID)], local_sem.at[3]),
        pltpu.make_async_copy(w_up, wgu.at[pl.ds(HID, HID)], local_sem.at[3]),
        pltpu.make_async_copy(w_down, wd, local_sem.at[4]),
    ]
    for load in loads:
        load.start()

    def expert_slots(e):
        return pl.ds(pl.multiple_of(e * PAD, PAD), PAD)

    def all_of(like, sem):
        pltpu.make_async_copy(like, like, sem).wait()


    def exchange(d):
        ex[d, r, expert_slots(g), :] = pick[d, expert_slots(g), :]
        for s in (4, 3, 5, 2, 6, 1, 7):
            pltpu.make_async_remote_copy(
                src_ref=pick.at[d, expert_slots(((y + s) % Y) // 2)],
                dst_ref=ex.at[d, r, expert_slots(g)],
                send_sem=small_send,
                recv_sem=ex_recv.at[d],
                device_id={"expert": columns[s]},
                device_id_type=MESH,
            ).start()

    def gather_own(d):
        all_of(meter.at[0], ex_recv.at[d])
        for half in range(2):
            rows[d, z, half] = dot_nn(packer, ex[d, half]).astype(BF16)
        if d == B:
            own_hop(0)
            other_hop(0)
        else:
            pass_on(d, 0, LONG)
            pass_on(d, 0, SHORT)
        absorb(d, ((z, 0), (z, 1)))

    ag_copies = {}
    paired = {}

    def send_piece(key, block, half, peer, sem):
        piece = rows.at[B, block, half]
        paired[key] = pltpu.make_async_remote_copy(
            src_ref=piece,
            dst_ref=piece,
            send_sem=ag_send,
            recv_sem=ag_recv.at[B, sem // 7, sem % 7],
            device_id={"expert": peer},
            device_id_type=MESH,
        )
        paired[key].start()

    def beside(way, distance):
        return (z + Z - distance) % Z if way == 0 else (z + distance) % Z

    def own_hop(hop):
        for way in range(2):
            if hop > 0:
                paired["own", way, hop - 1].wait_recv()
            if hop < 3:
                send_piece(("own", way, hop), beside(way, hop), r, up if way == 0 else down, way * 3 + hop)
            else:
                send_piece(("pair", way), beside(way, 3), r, partner, 10 + way)
        if hop == 3:
            send_piece("far", (z + 5 + 6 * r) % Z, r, up + r * (down - up), 12)

    def other_hop(hop):
        for way in range(2):
            if hop > 0:
                paired["other", way, hop - 1].wait_recv()
            if hop < 2:
                send_piece(("other", way, hop), beside(way, hop), 1 - r, up if way == 0 else down, 6 + way * 2 + hop)

    def arrived_kept(hop, chain):
        if chain == LONG and hop < 3:
            own_hop(hop + 1)
            absorb(B, [(beside(way, hop + 1), r) for way in range(2)])
        elif chain == LONG:
            paired["far"].wait_recv()
            send_piece("last", (z + 4) % Z, r, partner, 13)
            absorb(B, [((z + 4) % Z, r)])
        elif hop < 2:
            other_hop(hop + 1)
            absorb(B, [(beside(way, hop + 1), 1 - r) for way in range(2)])

    def arrived_pair():
        for way in range(2):
            paired["pair", way].wait_recv()
        absorb(B, [(beside(way, 3), 1 - r) for way in range(2)])
        paired["last"].wait_recv()
        absorb(B, [((z + 4) % Z, 1 - r)])

    def pass_on(d, hop, chain):
        for way in range(2):
            half = way if chain == LONG else 1 - way
            block = (z + Z - hop) % Z if way == 0 else (z + hop) % Z
            piece = rows.at[d, block, half]
            copy = pltpu.make_async_remote_copy(
                src_ref=piece,
                dst_ref=piece,
                send_sem=ag_send,
                recv_sem=ag_recv.at[d, way, chain + hop],
                device_id={"expert": up if way == 0 else down},
                device_id_type=MESH,
            )
            if hop > 0:
                ag_copies[d, way, hop - 1, chain].wait_recv()
            if hop == 2 and chain == LONG and d in DIRECT:
                skip(d, way)
            ag_copies[d, way, hop, chain] = copy
            copy.start()

    def skip(d, way):
        block = (z + Z - 2) % Z if way == 0 else (z + 2) % Z
        piece = rows.at[d, block, way]
        copy = pltpu.make_async_remote_copy(
            src_ref=piece,
            dst_ref=piece,
            send_sem=ag_send,
            recv_sem=ag_recv.at[d, way, LONG + 3],
            device_id={"expert": up_two if way == 0 else down_two},
            device_id_type=MESH,
        )
        ag_copies[d, way, 3, LONG] = copy
        copy.start()

    def features(block, half):
        return pl.ds(pl.multiple_of(half * HALF + block * DS, DS), DS)

    totals = {B: None, X: None, G: None}

    def absorb(d, blocks):
        for block, half in blocks:
            weights = wd if d == G else wgu
            term = dot_nt(rows[d, block, half], weights[:, features(block, half)])
            totals[d] = term if totals[d] is None else totals[d] + term

    def arrived(d, hop, chain):
        if d == B:
            arrived_kept(hop, chain)
            return
        if hop < 2 or (hop == 2 and chain == LONG and d not in DIRECT):
            pass_on(d, hop + 1, chain)
        else:
            for way in range(2):
                ag_copies[d, way, hop, chain].wait_recv()
        first, second = (0, 1) if chain == LONG else (1, 0)
        absorb(d, (((z + Z - hop - 1) % Z, first), ((z + hop + 1) % Z, second)))

    earlier[...] = before_mask()
    all_of(probs, local_sem.at[0])
    b_picker, b_column = pickers(routes[1], probs[1], g, earlier)
    loads[2].wait()
    pick[B] = dot_nn(b_picker, kept[...]).astype(BF16)
    pl.semaphore_wait(barrier, 13)

    relays = [
        pltpu.make_async_remote_copy(
            src_ref=source,
            dst_ref=relay.at[i],
            send_sem=relay_sem.at[i],
            recv_sem=relay_sem.at[2 + i],
            device_id={"section": peer},
            device_id_type=MESH,
        )
        for i, (source, peer) in enumerate(((acts, after), (grads, behind)))
    ]
    for copy in relays:
        copy.start()

    exchange(B)
    all_of(probs, local_sem.at[2])
    f_picker, f_column = pickers(routes[0], probs[0], g, earlier)

    relays[0].wait_recv()
    pick[X] = dot_nn(f_picker, relay[0]).astype(BF16)
    exchange(X)
    relays[1].wait_recv()
    pick[G] = (dot_nn(b_picker, relay[1]) * b_column).astype(BF16)
    exchange(G)

    packer = pack_matrix((ROWS, SLOTS), 1)
    unpacker = pack_matrix((SLOTS, ROWS), 0)
    token_of = [dot_tn(p, identity()).astype(BF16) for p in (f_picker, b_picker)]

    all_of(wgu, local_sem.at[3])
    all_of(wd, local_sem.at[4])

    gather_own(B)
    gather_own(X)
    arrived(B, 0, LONG)
    arrived(B, 0, SHORT)
    gather_own(G)
    for d, hop in ((X, 0), (B, 1), (G, 0), (X, 1), (B, 2), (G, 1), (X, 2)):
        arrived(d, hop, LONG)
        arrived(d, hop, SHORT)
    arrived(B, 3, LONG)
    arrived(G, 2, LONG)
    arrived(G, 2, SHORT)

    rs_copies = {}

    def own_part(c, block, half):
        if c == 0:
            return dot_nn(made[0], wd[:, features(block, half)])
        return dot_nn(made[1], wgu[:, features(block, half)])

    def turns(turn):
        if turn == 0:
            for way in range(2):
                yield way, way, 0
        for far in (0, 1):
            for way in range(2):
                yield way, way if far else 1 - way, turn + 1

    def part_of(way, step):
        return (z + 4 - step) % Z if way == 0 else (z + 4 + step) % Z

    def own_parts(c, turn):
        for way, half, step in turns(turn):
            parts[c, way, step, half] = own_part(c, part_of(way, step), half)

    def reduce_turn(c, turn):
        for way, half, step in turns(turn):
            value = parts[c, way, step, half] if turn > 0 else own_part(c, part_of(way, step), half)
            sources = (1, 0) if step == 2 and half == way else (step - 1,) if step > 1 else ()
            for source in sources:
                rs_copies[c, way, half, source].wait_recv()
                value = value + ring_in[c, way, source, half].astype(F32)
            ring_out[c, way, step, half] = value.astype(BF16)
            at = (c, way, step, half)
            next_one, next_two = (up, up_two) if way == 0 else (down, down_two)
            copy = pltpu.make_async_remote_copy(
                src_ref=ring_out.at[at],
                dst_ref=ring_in.at[at],
                send_sem=rs_send,
                recv_sem=rs_recv.at[c, way, step if half == way else 3 + step],
                device_id={"expert": next_two if step == 0 else next_one},
                device_id_type=MESH,
            )
            rs_copies[c, way, half, step] = copy
            copy.start()

    def send_back(c):
        mine = [own_part(c, z, half) for half in range(2)]
        for half in range(2):
            value = mine[half]
            for way in (1 - half, half):
                rs_copies[c, way, half, 3].wait_recv()
                value = value + ring_in[c, way, 3, half].astype(F32)
            fin[c, half] = dot_nn(unpacker, value.astype(BF16)).astype(BF16)
        comb[c, r, expert_slots(g), :] = fin[c, r, expert_slots(g), :]
        for s in (4, 3, 5, 2, 6, 1, 7):
            to = (y + s) % Y
            pltpu.make_async_remote_copy(
                src_ref=fin.at[c, to % 2, expert_slots(to // 2)],
                dst_ref=comb.at[c, r, expert_slots(g)],
                send_sem=small_send,
                recv_sem=fin_recv.at[c],
                device_id={"expert": columns[s]},
                device_id_type=MESH,
            ).start()

    def place(picker, values):
        high = values.astype(BF16)
        low = (values - high.astype(F32)).astype(BF16)
        return dot_nn(picker, high) + dot_nn(picker, low)

    def finish(c, picker, column, base, target):
        all_of(meter.at[0], fin_recv.at[c])
        values = comb[c, 0].astype(F32) + comb[c, 1].astype(F32)
        if column is not None:
            values = values * column
        target[...] = (base.astype(F32) + place(picker, values)).astype(BF16)

    made = {}

    arrived(X, 3, LONG)
    gate, upper = totals[X][:, :HID], totals[X][:, HID:]
    made[0] = (gate * jax.nn.sigmoid(gate) * upper).astype(BF16)
    reduce_turn(0, 0)
    arrived_pair()

    gate, upper = totals[B][:, :HID], totals[B][:, HID:]
    sig = jax.nn.sigmoid(gate)
    act = gate * sig
    slope = upper * sig * (1.0 + gate * (1.0 - sig))
    arrived(G, 3, LONG)
    d_hidden = totals[G]
    made[1] = jnp.concatenate([(d_hidden * slope).astype(BF16), (d_hidden * act).astype(BF16)], axis=1)
    reduce_turn(1, 0)
    for turn in range(1, 3):
        for c in range(2):
            own_parts(c, turn)
            reduce_turn(c, turn)
    send_back(0)
    send_back(1)
    finish(0, token_of[0], f_column, relay[0], out)
    finish(1, token_of[1], None, relay[1], out_grads)

    def drain():
        for copy in relays:
            copy.wait_send()
        all_of(meter, small_send)
        all_of(rows.at[:, pl.ds(0, 7)], ag_send)
        all_of(rows.at[pl.ds(0, 2), pl.ds(0, 7)], rs_send)

    drain()


def write_out(first, second, out, out_grads, sem):
    copies = [pltpu.make_async_copy(a, b, sem.at[i]) for i, (a, b) in enumerate(((first, out), (second, out_grads)))]
    for copy in copies:
        copy.start()
    for copy in copies:
        copy.wait()


def tick(section_acts, section_input_gradients, saved_input, fwd_routes, fwd_probs, back_routes, back_probs, w_gate, w_up, w_down):
    anywhere = pl.BlockSpec(memory_space=pl.ANY)
    inside = pl.BlockSpec(memory_space=pltpu.VMEM)
    block = pltpu.VMEM((TOK, DS), BF16)
    dma = pltpu.SemaphoreType.DMA
    out, out_grads = pl.pallas_call(
        kernel,
        out_shape=(block, block),
        in_specs=[anywhere] * 10,
        out_specs=(inside, inside),
        scratch_shapes=[
            pltpu.VMEM((2, TOK, DS), BF16),
            pltpu.VMEM((TOK, DS), BF16),
            pltpu.VMEM((2, TOP, E_WIN * TOK), jnp.int32),
            pltpu.VMEM((2, TOP, E_WIN * TOK), F32),
            pltpu.VMEM((2 * HID, 2 * HALF), BF16),
            pltpu.VMEM((HID, 2 * HALF), BF16),
            pltpu.VMEM((TOK, TOK), BF16),
            pltpu.VMEM((3, SLOTS, DS), BF16),
            pltpu.VMEM((3, 2, SLOTS, DS), BF16),
            pltpu.VMEM((3, Z, 2, ROWS, DS), BF16),
            pltpu.VMEM((2, 2, 4, 2, ROWS, DS), F32),
            pltpu.VMEM((2, 2, 4, 2, ROWS, DS), BF16),
            pltpu.VMEM((2, 2, 4, 2, ROWS, DS), BF16),
            pltpu.VMEM((2, 2, SLOTS, DS), BF16),
            pltpu.VMEM((2, 2, SLOTS, DS), BF16),
            pltpu.VMEM((5, 7, PAD, DS), BF16),
            dma((5,)),
            dma((4,)),
            dma,
            dma((3,)),
            dma,
            dma((3, 2, 7)),
            dma,
            dma((2, 2, 7)),
            dma((2,)),
        ],
        compiler_params=pltpu.CompilerParams(collective_id=0, has_side_effects=True),
    )(
        section_acts[0],
        section_input_gradients[0],
        saved_input[0],
        fwd_routes[0].T,
        fwd_probs[0].T,
        back_routes[0].T,
        back_probs[0].T,
        w_gate[0],
        w_up[0],
        w_down[0],
    )
    block = jax.ShapeDtypeStruct((TOK, DS), BF16)
    out, out_grads = pl.pallas_call(
        write_out,
        out_shape=(block, block),
        in_specs=[inside] * 2,
        out_specs=(anywhere, anywhere),
        scratch_shapes=[dma((2,))],
    )(*(pltpu.with_memory_space_constraint(v, pltpu.VMEM) for v in (out, out_grads)))
    return out[None], out_grads[None]


def solution(mesh):
    spread = P("section", "expert", None)
    whole = P("section", None, None)
    return jax.shard_map(
        tick,
        mesh=mesh,
        in_specs=(spread, spread, spread, whole, whole, whole, whole, spread, spread, spread),
        out_specs=(spread, spread),
        check_vma=False,
    )
```
